256 devices in a mesh: tile: 64 (over y, z, x_lo), sub: 4 (over x_hi, core).
Axes of the slice: x: 4 (x_hi: 2, x_lo: 2; x = x_hi * 2 + x_lo), y: 4, z: 8, core: 2. Of those that a mesh axis runs over, the one named last changes fastest.
Arguments:
- water_state: float32 [3, 512, 16384], P(None, 'tile', 'sub'), may hold values from -6 to 6
- water_coef: float32 [2, 512, 16384], P(None, 'tile', 'sub'), may hold values from 0.15 to 0.6
- steel_state: float32 [5, 1024, 16384], P(None, 'tile', 'sub'), may hold values from -6 to 6
- steel_coef: float32 [5, 1024, 16384], P(None, 'tile', 'sub'), may hold values from 0.15 to 0.6
- coupling: float32 [9], replicated, may hold values from 0.3 to 1.5
- water_cell: int32 [192, 1024], P('tile', 'sub'), may hold values from 0 to 32767, as said below
- stencil_code: int32 [192, 1024], P('tile', 'sub'), may hold values from 0 to 8
- link_count: int32 [192, 4], P('tile', 'sub'), may hold values from 0 to 256, as said below
- steel_cell: int32 [192, 1024], P('tile', 'sub'), may hold values from 4097 to 61438, as said below
Outputs:
- water_next: float32 [3, 512, 16384], P(None, 'tile', 'sub')
- steel_next: float32 [5, 1024, 16384], P(None, 'tile', 'sub')
The draws below stay inside these ranges and needn't reach their ends.
Inputs may be any that keep to these rules, and one draw needn't show every extreme that they name: `link_count`: entry [a * 3 + j, c] is the number of live leading slots of the list from water device (a, c) to steel device (a + j - 1, c); it is 0 where that tile does not exist, and for every water device one of its lists is full. `water_cell`: slots follow the interface curve: a few rows of each column near a profile that varies along the columns. `steel_cell`: entry [b * 3 + m, c * 256 + k] is row * 4096 + column in the block of steel device (b, c) that slot k of the list from water device (b + m - 1, c) reaches; it never lies in a block's outermost rows or columns.
All inputs are finite; a program needn't handle non-finite values.
Results may differ from the reference program's by a relative error of at most 0.00002.
Values sent between devices are 32-bit elements; how exact they have to be, the bound alone decides.
A program may use at most 64 MiB of HBM per device.

```python
import math
import jax
import jax.numpy as jnp

CXW = 8
CZW = 4096
CXS = 16
CZS = 4096
CAP = 256
STEPS = 3
TILES = 64
SUBS = 4
NXW = 512
NZW = 16384
NXS = 1024
NZS = 16384


def curve_rows(key, columns, width, lowest, highest):
    period = max(width // 2, 1)
    phase = jax.random.randint(jax.random.fold_in(key, 1), (TILES * 3, 1), 0, 2 * period)
    jitter = jax.random.randint(jax.random.fold_in(key, 2), columns.shape, 0, 2)
    wave = (columns + phase) % (2 * period)
    spread = highest - lowest
    rows = lowest + jnp.abs(wave - period) * spread // period + jitter
    return jnp.clip(rows, lowest, highest).astype(jnp.int32)


def draw_link_count(key, part):
    first_key = jax.random.fold_in(key, 11)
    second_key = jax.random.fold_in(key, 12)
    baseline = jax.random.randint(first_key, (TILES, 3, SUBS), CAP // 8, CAP // 2 + 1)
    pick = jax.random.randint(second_key, (TILES, 1, SUBS), 0, 3)
    tile_at = jnp.arange(TILES, dtype=jnp.int32)[:, None, None]
    offset = jnp.arange(3, dtype=jnp.int32)[None, :, None]
    bad_pick = (pick == 0) & (tile_at == 0) | (pick == 2) & (tile_at == TILES - 1)
    pick = jnp.where(bad_pick, 1, pick)
    counts = jnp.where(offset == pick, CAP, baseline)
    outside = (offset == 0) & (tile_at == 0) | (offset == 2) & (tile_at == TILES - 1)
    counts = jnp.where(outside, 0, counts)
    return counts.reshape(TILES * 3, SUBS).astype(jnp.int32)


def draw_water_cell(key, part):
    shape_two = (TILES * 3, SUBS * CAP)
    columns = jax.random.randint(jax.random.fold_in(key, 31), shape_two, 0, CZW)
    rows = curve_rows(jax.random.fold_in(key, 32), columns, CZW, 0, CXW - 1)
    cells = (rows * CZW + columns).astype(jnp.int32)
    cells = cells.at[0, 0].set(jnp.int32(0))
    cells = cells.at[0, 1].set(jnp.int32(CXW * CZW - 1))
    return cells.astype(jnp.int32)


def draw_steel_cell(key, part):
    shape_two = (TILES * 3, SUBS * CAP)
    columns = jax.random.randint(jax.random.fold_in(key, 21), shape_two, 1, CZS - 1)
    rows = curve_rows(jax.random.fold_in(key, 22), columns, CZS, 1, CXS - 2)
    cells = (rows * CZS + columns).astype(jnp.int32)
    cells = cells.at[0, 0].set(jnp.int32(CXS * CZS - CZS - 2))
    cells = cells.at[0, 1].set(jnp.int32(CZS + 1))
    return cells.astype(jnp.int32)


def with_ends(array, rng, least, largest):
    extent = array.shape
    index_at = [jax.random.randint(jax.random.fold_in(rng, axis), (), 0, extent[axis]) for axis in range(len(extent))]
    array = array.at[tuple(index_at)].set(least)
    longest = extent.index(max(extent))
    index_at[longest] = (index_at[longest] + 1) % extent[longest]
    return array.at[tuple(index_at)].set(largest)


def levels(own_key, shape, split, smallest, top_value):
    level = 1.0
    for position, blocks in split:
        draws = jax.random.uniform(jax.random.fold_in(jax.random.fold_in(own_key, 6), position), (blocks,), jnp.float32, smallest / len(split), top_value / len(split))
        level = level * jnp.repeat(jnp.exp(draws), shape[position] // blocks).reshape((-1,) + (1,) * (len(shape) - 1 - position))
    return level


def gaussian(stream_key, shape, scale, reach, cuts=(), kind=jnp.bfloat16):
    values = jax.random.normal(stream_key, shape, jnp.float32) * scale
    if len(cuts) > 0:
        values = levels(stream_key, shape, cuts, -0.22, 0.18) * values
    return jnp.clip(values, min=-reach, max=reach).astype(kind)


def setup_inputs(seed: int = 0) -> dict:
    key_of = jax.random.split(jax.random.key(seed), 10)
    water_state = gaussian(key_of[0], (3, NXW, NZW), 1.0, 6.0, ((1, 64), (2, 4)), jnp.float32)
    water_coef = jnp.clip(jnp.exp(math.log(0.6) - 1.3862944 * jax.random.uniform(key_of[1], (2, NXW, NZW), jnp.float32) ** levels(key_of[1], (2, NXW, NZW), ((1, 64), (2, 4)), -0.2, 0.2)), 0.15, 0.6)
    steel_state = gaussian(key_of[2], (5, NXS, NZS), 1.0, 6.0, ((1, 64), (2, 4)), jnp.float32)
    steel_coef = jnp.clip(jnp.exp(math.log(0.6) - 1.3862944 * jax.random.uniform(key_of[3], (5, NXS, NZS), jnp.float32) ** levels(key_of[3], (5, NXS, NZS), ((1, 64), (2, 4)), -0.2, 0.2)), 0.15, 0.6)
    coupling = jnp.clip(jnp.exp(jax.random.uniform(key_of[4], (9,), jnp.float32, math.log(0.3), math.log(1.5))), 0.3, 1.5)
    water_cell = draw_water_cell(jax.random.fold_in(key_of[9], 71), 0)
    stencil_code = with_ends(jax.random.randint(key_of[6], (TILES * 3, SUBS * CAP), 0, 9), jax.random.fold_in(key_of[6], 1), 0, 8).astype(jnp.int32)
    link_count = draw_link_count(jax.random.fold_in(key_of[9], 71), 0)
    steel_cell = draw_steel_cell(jax.random.fold_in(key_of[9], 71), 0)
    return dict(water_state=water_state, water_coef=water_coef, steel_state=steel_state, steel_coef=steel_coef, coupling=coupling, water_cell=water_cell, stencil_code=stencil_code, link_count=link_count, steel_cell=steel_cell)


def across_rows(field):
    padded = jnp.pad(field, ((1, 1), (0, 0)))
    return 0.5 * (padded[2:] - padded[:-2])


def across_columns(field):
    padded = jnp.pad(field, ((0, 0), (1, 1)))
    return 0.5 * (padded[:, 2:] - padded[:, :-2])


def reference(water_state, water_coef, steel_state, steel_coef, coupling, water_cell, stencil_code, link_count, steel_cell):
    shape_four = (TILES, 3, SUBS, CAP)
    leading = jnp.arange(TILES, dtype=jnp.int32)[:, None, None, None]
    offsets = jnp.arange(3, dtype=jnp.int32)[None, :, None, None]
    subgrid = jnp.arange(SUBS, dtype=jnp.int32)[None, None, :, None]
    slot_index = jnp.arange(CAP, dtype=jnp.int32)[None, None, None, :]
    counts = link_count.reshape(TILES, 3, SUBS)[..., None]
    live = (slot_index < counts).astype(jnp.float32)
    factor = coupling[stencil_code.reshape(shape_four)] * live
    water_index = water_cell.reshape(shape_four)
    water_rows = (leading * CXW + water_index // CZW).astype(jnp.int32)
    water_columns = (subgrid * CZW + water_index % CZW).astype(jnp.int32)
    target = jnp.clip(leading + offsets - 1, 0, TILES - 1).astype(jnp.int32)
    steel_four = steel_cell.reshape(shape_four)
    steel_index = steel_four[target, (2 - offsets).astype(jnp.int32), subgrid, slot_index]
    steel_rows = (target * CXS + steel_index // CZS).astype(jnp.int32)
    steel_columns = (subgrid * CZS + steel_index % CZS).astype(jnp.int32)
    for time_step in range(STEPS):
        pressure = water_state[0]
        velocity_x = water_state[1]
        velocity_z = water_state[2]
        sample = pressure[water_rows, water_columns] * factor
        loading = jnp.zeros((NXS, NZS), jnp.float32).at[steel_rows, steel_columns].add(sample)
        buoyancy = steel_coef[0]
        steel_ux = steel_state[0] + buoyancy * (across_rows(steel_state[2]) + across_columns(steel_state[4]))
        steel_uz = steel_state[1] + buoyancy * ((across_rows(steel_state[4]) + across_columns(steel_state[3])) - loading)
        stress_xx = steel_state[2] + steel_coef[1] * across_rows(steel_ux) + steel_coef[2] * across_columns(steel_uz)
        stress_zz = steel_state[3] + steel_coef[2] * across_rows(steel_ux) + steel_coef[3] * across_columns(steel_uz)
        stress_xz = steel_state[4] + steel_coef[4] * (across_columns(steel_ux) + across_rows(steel_uz))
        steel_state = jnp.stack([steel_ux, steel_uz, stress_xx, stress_zz, stress_xz])
        traction = stress_zz[steel_rows, steel_columns] * factor
        feeding = jnp.zeros((NXW, NZW), jnp.float32).at[water_rows, water_columns].add(traction)
        new_vx = velocity_x - water_coef[0] * across_rows(pressure)
        new_vz = velocity_z - water_coef[0] * across_columns(pressure)
        new_pressure = pressure - water_coef[1] * (across_rows(new_vx) + across_columns(new_vz)) + feeding
        water_state = jnp.stack([new_pressure, new_vx, new_vz])
    return water_state, steel_state
```

```python
import functools

import jax
import jax.numpy as jnp
from jax import lax
from jax.experimental import pallas as pl
from jax.experimental.pallas import tpu as pltpu
from jax.sharding import PartitionSpec as P

MESH = pl.DeviceIdType.MESH
STEPS = 3
LANES = 128
F32 = jnp.float32
BF16 = jnp.bfloat16


def split_two(x):
    first = x.astype(BF16)
    return first, (x - first.astype(F32)).astype(BF16)


class Columns:
    def __init__(self, get, left, right, count, shape):
        self.get, self.left, self.right, self.count = get, left, right, count
        lane = lax.broadcasted_iota(jnp.int32, shape, 1)
        self.is_first, self.is_last = lane == 0, lane == LANES - 1
        self.before, self.after = {}, {}

    def tile(self, h):
        return self.left() if h < 0 else self.right() if h == self.count else self.get(h)

    def rolled(self, h, cache, shift):
        if h not in cache:
            cache[h] = pltpu.roll(self.tile(h), shift, 1)
        return cache[h]

    def __call__(self, h):
        previous = jnp.where(
            self.is_first, self.rolled(h - 1, self.before, 1), self.rolled(h, self.before, 1)
        )
        following = jnp.where(
            self.is_last,
            self.rolled(h + 1, self.after, LANES - 1),
            self.rolled(h, self.after, LANES - 1),
        )
        return following - previous


def row_difference(tile, above, below, is_top, is_bottom):
    rows = tile.shape[0]
    previous = jnp.where(is_top, above, pltpu.roll(tile, 1, 0))
    following = jnp.where(is_bottom, below, pltpu.roll(tile, rows - 1, 0))
    return following - previous


def kernel(
    dims,
    coupling,
    counts,
    water_cell,
    stencil_code,
    steel_cell,
    water_in,
    water_coef_in,
    steel_in,
    steel_coef_in,
    water_out,
    steel_out,
    W,
    WC,
    S,
    SC,
    RW,
    RS,
    LW,
    LS,
    FAC,
    LOAD,
    lists_out,
    lists_in,
    stress_rows_out,
    stress_rows_in,
    speed_rows_out,
    speed_rows_in,
    p_rows_out,
    p_rows_in,
    vx_rows_out,
    vx_rows_in,
    stress_cols_in,
    speed_cols_in,
    p_cols_in,
    vz_cols_in,
    local_sem,
    send_sem,
    recv_sem,
):
    tiles, subs, rw, rs, nz, cap = dims
    nh = nz // LANES
    shift = nz.bit_length() - 1
    slots = 3 * cap
    a = lax.axis_index("tile")
    c = lax.axis_index("sub")
    has = (a > 0, a < tiles - 1, c > 0, c < subs - 1)
    target = ((a - 1, c), (a + 1, c), (a, c - 1), (a, c + 1))

    barrier = pltpu.get_barrier_semaphore()
    for d in range(4):

        @pl.when(has[d])
        def _():
            pl.semaphore_signal(barrier, inc=1, device_id=target[d], device_id_type=MESH)

    loads = [
        pltpu.make_async_copy(src, dst, local_sem.at[i])
        for i, (src, dst) in enumerate(
            ((water_in, W), (steel_in, S), (water_coef_in, WC), (steel_coef_in, SC))
        )
    ]
    for load in loads:
        load.start()

    ids = {}

    def copy(name, d, src, dst):
        key = (name, d)
        if key not in ids:
            ids[key] = len(ids)
        return pltpu.make_async_remote_copy(
            src_ref=src,
            dst_ref=dst,
            send_sem=send_sem.at[ids[key]],
            recv_sem=recv_sem.at[ids[key]],
            device_id=target[d],
            device_id_type=MESH,
        )

    pending = {}

    def send(name, d, src, dst):
        @pl.when(has[d])
        def _():
            copy(name, d, src, dst).start()

        pending[(name, d)] = (src, dst)

    def arrived(name, d, dst):
        @pl.when(has[d ^ 1])
        def _():
            copy(name, d, dst, dst).wait_recv()

    def sent(name, d):
        src, dst = pending.pop((name, d))

        @pl.when(has[d])
        def _():
            copy(name, d, src, dst).wait_send()

    for d, refs in (
        (0, (lists_in, stress_rows_in, speed_rows_in, p_rows_in, vx_rows_in)),
        (1, (lists_in, stress_rows_in, speed_rows_in, p_rows_in, vx_rows_in)),
        (2, (stress_cols_in, speed_cols_in, p_cols_in, vz_cols_in)),
        (3, (stress_cols_in, speed_cols_in, p_cols_in, vz_cols_in)),
    ):

        @pl.when(jnp.logical_not(has[d ^ 1]))
        def _():
            for ref in refs:
                part = ref.at[d % 2]
                part[...] = jnp.zeros(part.shape, F32)

    lane_row = lambda ref: jnp.concatenate([ref[0:1, :], ref[1:2, :], ref[2:3, :]], axis=1)
    wcell = lane_row(water_cell)
    scell = lane_row(steel_cell)
    code = lane_row(stencil_code)
    slot = lax.broadcasted_iota(jnp.int32, (1, cap), 1)
    live = jnp.concatenate([slot < counts[m, 0] for m in range(3)], axis=1)
    weight = jnp.zeros((1, slots), F32)
    for k in range(9):
        weight = jnp.where(code == k, coupling[k], weight)
    FAC[...] = jnp.where(live, weight, 0.0)

    def selectors(cell, rows, R, L):
        row = cell >> shift
        key = ((cell >> 7) & (nh - 1)) * rows + row
        low = cell & (LANES - 1)
        count = nh * rows
        block = min(128, count)
        for k0 in range(0, count, block):
            index = lax.broadcasted_iota(jnp.int32, (block, slots), 0) + k0
            R[k0 : k0 + block, :] = jnp.where(index == key, 1.0, 0.0).astype(BF16)
        index = lax.broadcasted_iota(jnp.int32, (LANES, slots), 0)
        L[...] = jnp.where(index == low, 1.0, 0.0)

    selectors(wcell, rw, RW, LW)

    def gather(field, rows, R, L):
        stacked = jnp.concatenate(
            [field[:, h * LANES : (h + 1) * LANES] for h in range(nh)], axis=0
        )
        parts = split_two(jnp.transpose(stacked))
        picked = jnp.dot(
            jnp.concatenate(parts, axis=0), R[...], preferred_element_type=F32
        )
        picked = (picked[:LANES] + picked[LANES:]) * L[...]
        return jnp.sum(picked, axis=0, keepdims=True)

    def scatter(values, R, L):
        parts = split_two(L[...] * values)
        spread = lax.dot_general(
            R[...],
            jnp.concatenate(parts, axis=0),
            (((1,), (1,)), ((), ())),
            preferred_element_type=F32,
        )
        return spread[:, :LANES] + spread[:, LANES:]

    def masks(rows):
        row = lax.broadcasted_iota(jnp.int32, (rows, LANES), 0)
        return row == 0, row == rows - 1

    steel_top, steel_bottom = masks(rs)
    water_top, water_bottom = masks(rw)
    at = lambda h: slice(h * LANES, (h + 1) * LANES)

    def send_lists(name, n, values):
        lists_out[0, n] = values[:, :cap]
        lists_out[1, n] = values[:, 2 * cap :]
        for d in (0, 1):
            send(name, d, lists_out.at[d, n], lists_in.at[d, n])

    def receive_lists(name, n, values):
        for d in (0, 1):
            arrived(name, d, lists_in.at[d, n])
        return jnp.concatenate(
            [lists_in[1, n], values[:, cap : 2 * cap], lists_in[0, n]], axis=1
        )

    def send_rows(name, n, fields, rows, out, into):
        for d, r in ((0, 0), (1, rows - 1)):
            for i, (ref, f) in enumerate(fields):
                out[d, n, i] = ref[f, r : r + 1, :]
            send(name, d, out.at[d, n], into.at[d, n])

    def send_cols(name, n, src, into):
        send(name, 2, src[0], into.at[0, n])
        send(name, 3, src[1], into.at[1, n])

    def wait_rows(name, n, into):
        for d in (0, 1):
            arrived(name, d, into.at[d, n])

    def wait_cols(name, n, into):
        for d in (2, 3):
            arrived(name, d, into.at[d - 2, n])

    def all_sent(name, directions):
        for d in directions:
            sent(name, d)

    first, last = slice(0, LANES), slice(nz - LANES, nz)

    def send_stress(n):
        send_rows(f"sr{n}", n, ((S, 2), (S, 4)), rs, stress_rows_out, stress_rows_in)
        send_cols(f"sc{n}", n, (S.at[3:5, :, first], S.at[3:5, :, last]), stress_cols_in)

    def send_speed(n):
        send_rows(f"ur{n}", n, ((S, 0), (S, 1)), rs, speed_rows_out, speed_rows_in)
        send_cols(f"uc{n}", n, (S.at[0:2, :, first], S.at[0:2, :, last]), speed_cols_in)

    def send_p(n):
        send_rows(f"pr{n}", n, ((W, 0),), rw, p_rows_out, p_rows_in)
        send_cols(f"pc{n}", n, (W.at[0, :, first], W.at[0, :, last]), p_cols_in)

    def send_v(n):
        send_rows(f"vr{n}", n, ((W, 1),), rw, vx_rows_out, vx_rows_in)
        send_cols(f"vc{n}", n, (W.at[2, :, first], W.at[2, :, last]), vz_cols_in)

    def columns(ref, f, into, n, i, rows):
        return Columns(
            lambda h: ref[f, :, at(h)],
            (lambda: into[1, n]) if i is None else (lambda: into[1, n, i]),
            (lambda: into[0, n]) if i is None else (lambda: into[0, n, i]),
            nh,
            (rows, LANES),
        )

    def rows_of(ref, f, into, n, i, top, bottom):
        return lambda h: row_difference(
            ref[f, :, at(h)], into[1, n, i, :, at(h)], into[0, n, i, :, at(h)], top, bottom
        )

    def steel_speed(n):
        wait_rows(f"sr{n}", n, stress_rows_in)
        wait_cols(f"sc{n}", n, stress_cols_in)
        dr_xx = rows_of(S, 2, stress_rows_in, n, 0, steel_top, steel_bottom)
        dr_xz = rows_of(S, 4, stress_rows_in, n, 1, steel_top, steel_bottom)
        dc_zz = columns(S, 3, stress_cols_in, n, 0, rs)
        dc_xz = columns(S, 4, stress_cols_in, n, 1, rs)
        for h in range(nh):
            half = 0.5 * SC[0, :, at(h)]
            S[0, :, at(h)] = S[0, :, at(h)] + half * (dr_xx(h) + dc_xz(h))
            S[1, :, at(h)] = S[1, :, at(h)] + half * (dr_xz(h) + dc_zz(h))

    def steel_load(values):
        LOAD[...] = scatter(values, RS, LS)
        for h in range(nh):
            S[1, :, at(h)] = S[1, :, at(h)] - SC[0, :, at(h)] * LOAD[h * rs : (h + 1) * rs, :]

    def steel_stress(n):
        wait_rows(f"ur{n}", n, speed_rows_in)
        wait_cols(f"uc{n}", n, speed_cols_in)
        dr_x = rows_of(S, 0, speed_rows_in, n, 0, steel_top, steel_bottom)
        dr_z = rows_of(S, 1, speed_rows_in, n, 1, steel_top, steel_bottom)
        dc_x = columns(S, 0, speed_cols_in, n, 0, rs)
        dc_z = columns(S, 1, speed_cols_in, n, 1, rs)
        for h in range(nh):
            across, along = 0.5 * dr_x(h), 0.5 * dc_z(h)
            S[2, :, at(h)] = S[2, :, at(h)] + SC[1, :, at(h)] * across + SC[2, :, at(h)] * along
            S[3, :, at(h)] = S[3, :, at(h)] + SC[2, :, at(h)] * across + SC[3, :, at(h)] * along
            S[4, :, at(h)] = S[4, :, at(h)] + (0.5 * SC[4, :, at(h)]) * (dc_x(h) + dr_z(h))

    def water_speed(n):
        wait_rows(f"pr{n}", n, p_rows_in)
        wait_cols(f"pc{n}", n, p_cols_in)
        dr_p = rows_of(W, 0, p_rows_in, n, 0, water_top, water_bottom)
        dc_p = columns(W, 0, p_cols_in, n, None, rw)
        for h in range(nh):
            half = 0.5 * WC[0, :, at(h)]
            W[1, :, at(h)] = W[1, :, at(h)] - half * dr_p(h)
            W[2, :, at(h)] = W[2, :, at(h)] - half * dc_p(h)

    def water_pressure(n):
        wait_rows(f"vr{n}", n, vx_rows_in)
        wait_cols(f"vc{n}", n, vz_cols_in)
        dr_v = rows_of(W, 1, vx_rows_in, n, 0, water_top, water_bottom)
        dc_v = columns(W, 2, vz_cols_in, n, None, rw)
        for h in range(nh):
            W[0, :, at(h)] = W[0, :, at(h)] - (0.5 * WC[1, :, at(h)]) * (dr_v(h) + dc_v(h))

    def water_feed(values):
        fed = scatter(values * FAC[...], RW, LW)
        for h in range(nh):
            W[0, :, at(h)] = W[0, :, at(h)] + fed[h * rw : (h + 1) * rw, :]

    loads[0].wait()
    sample = gather(W.at[0], rw, RW, LW) * FAC[...]
    loads[1].wait()
    pl.semaphore_wait(barrier, sum(h.astype(jnp.int32) for h in has))

    send_stress(0)
    send_lists("s0", 0, sample)
    send_p(0)
    selectors(scell, rs, RS, LS)
    loads[2].wait()
    loads[3].wait()
    for n in range(STEPS):
        steel_speed(n)
        send_speed(n)
        water_speed(n)
        send_v(n)
        all_sent(f"sr{n}", (0, 1))
        all_sent(f"sc{n}", (2, 3))
        all_sent(f"pr{n}", (0, 1))
        all_sent(f"pc{n}", (2, 3))
        steel_load_values = receive_lists(f"s{n}", 2 * n, sample)
        all_sent(f"uc{n}", (2, 3))
        steel_load(steel_load_values)
        steel_stress(n)
        traction = gather(S.at[3], rs, RS, LS)
        send_lists(f"t{n}", 2 * n + 1, traction)
        if n < STEPS - 1:
            send_stress(n + 1)
        water_pressure(n)
        returning = receive_lists(f"t{n}", 2 * n + 1, traction)
        water_feed(returning)
        if n < STEPS - 1:
            sample = gather(W.at[0], rw, RW, LW) * FAC[...]
            send_lists(f"s{n + 1}", 2 * n + 2, sample)
            send_p(n + 1)
        all_sent(f"s{n}", (0, 1))
        all_sent(f"t{n}", (0, 1))
        all_sent(f"ur{n}", (0, 1))
        all_sent(f"vr{n}", (0, 1))
        all_sent(f"vc{n}", (2, 3))
    stores = [
        pltpu.make_async_copy(W, water_out, local_sem.at[0]),
        pltpu.make_async_copy(S, steel_out, local_sem.at[1]),
    ]
    for store in stores:
        store.start()
    for store in stores:
        store.wait()


def on_device(
    tiles,
    subs,
    water_state,
    water_coef,
    steel_state,
    steel_coef,
    coupling,
    water_cell,
    stencil_code,
    link_count,
    steel_cell,
):
    rw, nz = water_state.shape[1:]
    rs = steel_state.shape[1]
    cap = water_cell.shape[1]
    slots = 3 * cap
    nh = nz // LANES
    vmem = pl.BlockSpec(memory_space=pltpu.VMEM)
    smem = pl.BlockSpec(memory_space=pltpu.SMEM)
    anywhere = pl.BlockSpec(memory_space=pl.ANY)
    rows_of = lambda fields: pltpu.VMEM((2, STEPS, fields, 1, nz), F32)
    return pl.pallas_call(
        functools.partial(kernel, (tiles, subs, rw, rs, nz, cap)),
        out_shape=(
            jax.ShapeDtypeStruct(water_state.shape, F32),
            jax.ShapeDtypeStruct(steel_state.shape, F32),
        ),
        in_specs=[smem, smem, vmem, vmem, vmem] + [anywhere] * 4,
        out_specs=(anywhere, anywhere),
        scratch_shapes=[
            pltpu.VMEM(water_state.shape, F32),
            pltpu.VMEM(water_coef.shape, F32),
            pltpu.VMEM(steel_state.shape, F32),
            pltpu.VMEM(steel_coef.shape, F32),
            pltpu.VMEM((nh * rw, slots), BF16),
            pltpu.VMEM((nh * rs, slots), BF16),
            pltpu.VMEM((LANES, slots), F32),
            pltpu.VMEM((LANES, slots), F32),
            pltpu.VMEM((1, slots), F32),
            pltpu.VMEM((nh * rs, LANES), F32),
            pltpu.VMEM((2, 2 * STEPS, 1, cap), F32),
            pltpu.VMEM((2, 2 * STEPS, 1, cap), F32),
            rows_of(2),
            rows_of(2),
            rows_of(2),
            rows_of(2),
            rows_of(1),
            rows_of(1),
            rows_of(1),
            rows_of(1),
            pltpu.VMEM((2, STEPS, 2, rs, LANES), F32),
            pltpu.VMEM((2, STEPS, 2, rs, LANES), F32),
            pltpu.VMEM((2, STEPS, rw, LANES), F32),
            pltpu.VMEM((2, STEPS, rw, LANES), F32),
            pltpu.SemaphoreType.DMA((4,)),
            pltpu.SemaphoreType.DMA((64,)),
            pltpu.SemaphoreType.DMA((64,)),
        ],
        compiler_params=pltpu.CompilerParams(
            collective_id=0, has_side_effects=True, vmem_limit_bytes=48 * 1024 * 1024
        ),
    )(
        coupling,
        link_count,
        water_cell,
        stencil_code,
        steel_cell,
        water_state,
        water_coef,
        steel_state,
        steel_coef,
    )


def solution(mesh):
    in_specs = (
        P(None, "tile", "sub"),
        P(None, "tile", "sub"),
        P(None, "tile", "sub"),
        P(None, "tile", "sub"),
        P(),
        P("tile", "sub"),
        P("tile", "sub"),
        P("tile", "sub"),
        P("tile", "sub"),
    )
    out_specs = (P(None, "tile", "sub"), P(None, "tile", "sub"))
    return jax.shard_map(
        functools.partial(on_device, mesh.shape["tile"], mesh.shape["sub"]),
        mesh=mesh,
        in_specs=in_specs,
        out_specs=out_specs,
        check_vma=False,
    )
```

```python
import functools

import jax
import jax.numpy as jnp
from jax import lax
from jax.experimental import pallas as pl
from jax.experimental.pallas import tpu as pltpu
from jax.sharding import PartitionSpec as P

MESH = pl.DeviceIdType.MESH
STEPS = 3
LANES = 128
VMEM_BYTES = 67043328
F32 = jnp.float32
BF16 = jnp.bfloat16


def split_two(x):
    first = x.astype(BF16)
    return first, (x - first.astype(F32)).astype(BF16)


class Columns:
    def __init__(self, get, left, right, count, shape):
        self.get, self.left, self.right, self.count = get, left, right, count
        lane = lax.broadcasted_iota(jnp.int32, shape, 1)
        self.is_first, self.is_last = lane == 0, lane == LANES - 1
        self.before, self.after = {}, {}

    def tile(self, h):
        return self.left() if h < 0 else self.right() if h == self.count else self.get(h)

    def rolled(self, h, cache, shift):
        if h not in cache:
            cache[h] = pltpu.roll(self.tile(h), shift, 1)
        return cache[h]

    def __call__(self, h):
        previous = jnp.where(
            self.is_first, self.rolled(h - 1, self.before, 1), self.rolled(h, self.before, 1)
        )
        following = jnp.where(
            self.is_last,
            self.rolled(h + 1, self.after, LANES - 1),
            self.rolled(h, self.after, LANES - 1),
        )
        return following - previous


def row_difference(tile, above, below, is_top, is_bottom):
    rows = tile.shape[0]
    previous = jnp.where(is_top, above, pltpu.roll(tile, 1, 0))
    following = jnp.where(is_bottom, below, pltpu.roll(tile, rows - 1, 0))
    return following - previous


def kernel(
    dims,
    coupling_in,
    counts_in,
    water_cell_in,
    stencil_code_in,
    steel_cell_in,
    water_in,
    water_coef_in,
    steel_in,
    steel_coef_in,
    W,
    S,
    coupling,
    counts,
    water_cell,
    stencil_code,
    steel_cell,
    WC,
    SC,
    RW,
    RS,
    LW,
    LS,
    FAC,
    LOAD,
    lists_out,
    lists_in,
    stress_rows_out,
    stress_rows_in,
    speed_rows_out,
    speed_rows_in,
    p_rows_out,
    p_rows_in,
    vx_rows_out,
    vx_rows_in,
    stress_cols_in,
    speed_cols_in,
    p_cols_in,
    vz_cols_in,
    local_sem,
    send_sem,
    recv_sem,
):
    tiles, subs, rw, rs, nz, cap = dims
    nh = nz // LANES
    shift = nz.bit_length() - 1
    slots = 3 * cap
    a = lax.axis_index("tile")
    c = lax.axis_index("sub")
    has = (a > 0, a < tiles - 1, c > 0, c < subs - 1)
    target = ((a - 1, c), (a + 1, c), (a, c - 1), (a, c + 1))

    barrier = pltpu.get_barrier_semaphore()
    for d in range(4):

        @pl.when(has[d])
        def _():
            pl.semaphore_signal(barrier, inc=1, device_id=target[d], device_id_type=MESH)

    loads = [
        pltpu.make_async_copy(src, dst, local_sem.at[i])
        for i, (src, dst) in enumerate(
            (
                (coupling_in, coupling),
                (counts_in, counts),
                (stencil_code_in, stencil_code),
                (water_cell_in, water_cell),
                (water_in, W),
                (steel_cell_in, steel_cell),
                (steel_in, S),
                (water_coef_in, WC),
                (steel_coef_in, SC),
            )
        )
    ]
    for load in loads:
        load.start()

    ids = {}

    def copy(name, d, src, dst):
        key = (name, d)
        if key not in ids:
            ids[key] = len(ids)
        return pltpu.make_async_remote_copy(
            src_ref=src,
            dst_ref=dst,
            send_sem=send_sem.at[ids[key]],
            recv_sem=recv_sem.at[ids[key]],
            device_id=target[d],
            device_id_type=MESH,
        )

    pending = {}

    def send(name, d, src, dst):
        @pl.when(has[d])
        def _():
            copy(name, d, src, dst).start()

        pending[(name, d)] = (src, dst)

    def arrived(name, d, dst):
        @pl.when(has[d ^ 1])
        def _():
            copy(name, d, dst, dst).wait_recv()

    def sent(name, d):
        src, dst = pending.pop((name, d))

        @pl.when(has[d])
        def _():
            copy(name, d, src, dst).wait_send()

    for d, refs in (
        (0, (lists_in, stress_rows_in, speed_rows_in, p_rows_in, vx_rows_in)),
        (1, (lists_in, stress_rows_in, speed_rows_in, p_rows_in, vx_rows_in)),
        (2, (stress_cols_in, speed_cols_in, p_cols_in, vz_cols_in)),
        (3, (stress_cols_in, speed_cols_in, p_cols_in, vz_cols_in)),
    ):

        @pl.when(jnp.logical_not(has[d ^ 1]))
        def _():
            for ref in refs:
                part = ref.at[d % 2]
                part[...] = jnp.zeros(part.shape, F32)

    for load in loads[:4]:
        load.wait()
    lane_row = lambda ref: jnp.concatenate([ref[0:1, :], ref[1:2, :], ref[2:3, :]], axis=1)
    wcell = lane_row(water_cell)
    code = lane_row(stencil_code)
    slot = lax.broadcasted_iota(jnp.int32, (1, cap), 1)
    live = jnp.concatenate([slot < counts[0, m] for m in range(3)], axis=1)
    weight = jnp.zeros((1, slots), F32)
    for k in range(9):
        weight = jnp.where(code == k, coupling[k], weight)
    FAC[...] = jnp.where(live, weight, 0.0)

    def selectors(cell, rows, R, L):
        row = cell >> shift
        key = ((cell >> 7) & (nh - 1)) * rows + row
        low = cell & (LANES - 1)
        count = nh * rows
        block = min(128, count)
        for k0 in range(0, count, block):
            index = lax.broadcasted_iota(jnp.int32, (block, slots), 0) + k0
            R[k0 : k0 + block, :] = jnp.where(index == key, 1.0, 0.0).astype(BF16)
        index = lax.broadcasted_iota(jnp.int32, (LANES, slots), 0)
        L[...] = jnp.where(index == low, 1.0, 0.0)

    selectors(wcell, rw, RW, LW)

    def gather(field, rows, R, L):
        stacked = jnp.concatenate(
            [field[:, h * LANES : (h + 1) * LANES] for h in range(nh)], axis=0
        )
        parts = split_two(jnp.transpose(stacked))
        picked = jnp.dot(
            jnp.concatenate(parts, axis=0), R[...], preferred_element_type=F32
        )
        picked = (picked[:LANES] + picked[LANES:]) * L[...]
        return jnp.sum(picked, axis=0, keepdims=True)

    def scatter(values, R, L):
        parts = split_two(L[...] * values)
        spread = lax.dot_general(
            R[...],
            jnp.concatenate(parts, axis=0),
            (((1,), (1,)), ((), ())),
            preferred_element_type=F32,
        )
        return spread[:, :LANES] + spread[:, LANES:]

    def masks(rows):
        row = lax.broadcasted_iota(jnp.int32, (rows, LANES), 0)
        return row == 0, row == rows - 1

    steel_top, steel_bottom = masks(rs)
    water_top, water_bottom = masks(rw)
    at = lambda h: slice(h * LANES, (h + 1) * LANES)

    def send_lists(name, n, values):
        lists_out[0, n] = values[:, :cap]
        lists_out[1, n] = values[:, 2 * cap :]
        for d in (0, 1):
            send(name, d, lists_out.at[d, n], lists_in.at[d, n])

    def receive_lists(name, n, values):
        for d in (0, 1):
            arrived(name, d, lists_in.at[d, n])
        return jnp.concatenate(
            [lists_in[1, n], values[:, cap : 2 * cap], lists_in[0, n]], axis=1
        )

    def send_rows(name, n, fields, rows, out, into):
        for d, r in ((0, 0), (1, rows - 1)):
            for i, (ref, f) in enumerate(fields):
                out[d, n, i] = ref[f, r : r + 1, :]
            send(name, d, out.at[d, n], into.at[d, n])

    def send_cols(name, n, src, into):
        send(name, 2, src[0], into.at[0, n])
        send(name, 3, src[1], into.at[1, n])

    def wait_rows(name, n, into):
        for d in (0, 1):
            arrived(name, d, into.at[d, n])

    def wait_cols(name, n, into):
        for d in (2, 3):
            arrived(name, d, into.at[d - 2, n])

    def all_sent(name, directions):
        for d in directions:
            sent(name, d)

    first, last = slice(0, LANES), slice(nz - LANES, nz)

    def send_stress(n):
        send_rows(f"sr{n}", n, ((S, 2), (S, 4)), rs, stress_rows_out, stress_rows_in)
        send_cols(f"sc{n}", n, (S.at[3:5, :, first], S.at[3:5, :, last]), stress_cols_in)

    def send_speed(n):
        send_rows(f"ur{n}", n, ((S, 0), (S, 1)), rs, speed_rows_out, speed_rows_in)
        send_cols(f"uc{n}", n, (S.at[0:2, :, first], S.at[0:2, :, last]), speed_cols_in)

    def send_p(n):
        send_rows(f"pr{n}", n, ((W, 0),), rw, p_rows_out, p_rows_in)
        send_cols(f"pc{n}", n, (W.at[0, :, first], W.at[0, :, last]), p_cols_in)

    def send_v(n):
        send_rows(f"vr{n}", n, ((W, 1),), rw, vx_rows_out, vx_rows_in)
        send_cols(f"vc{n}", n, (W.at[2, :, first], W.at[2, :, last]), vz_cols_in)

    def columns(ref, f, into, n, i, rows):
        return Columns(
            lambda h: ref[f, :, at(h)],
            (lambda: into[1, n]) if i is None else (lambda: into[1, n, i]),
            (lambda: into[0, n]) if i is None else (lambda: into[0, n, i]),
            nh,
            (rows, LANES),
        )

    def rows_of(ref, f, into, n, i, top, bottom):
        return lambda h: row_difference(
            ref[f, :, at(h)], into[1, n, i, :, at(h)], into[0, n, i, :, at(h)], top, bottom
        )

    def steel_speed(n):
        wait_rows(f"sr{n}", n, stress_rows_in)
        wait_cols(f"sc{n}", n, stress_cols_in)
        dr_xx = rows_of(S, 2, stress_rows_in, n, 0, steel_top, steel_bottom)
        dr_xz = rows_of(S, 4, stress_rows_in, n, 1, steel_top, steel_bottom)
        dc_zz = columns(S, 3, stress_cols_in, n, 0, rs)
        dc_xz = columns(S, 4, stress_cols_in, n, 1, rs)
        for h in range(nh):
            half = 0.5 * SC[0, :, at(h)]
            S[0, :, at(h)] = S[0, :, at(h)] + half * (dr_xx(h) + dc_xz(h))
            S[1, :, at(h)] = S[1, :, at(h)] + half * (dr_xz(h) + dc_zz(h))

    def steel_load(values):
        LOAD[...] = scatter(values, RS, LS)
        for h in range(nh):
            S[1, :, at(h)] = S[1, :, at(h)] - SC[0, :, at(h)] * LOAD[h * rs : (h + 1) * rs, :]

    def steel_stress(n):
        wait_rows(f"ur{n}", n, speed_rows_in)
        wait_cols(f"uc{n}", n, speed_cols_in)
        dr_x = rows_of(S, 0, speed_rows_in, n, 0, steel_top, steel_bottom)
        dr_z = rows_of(S, 1, speed_rows_in, n, 1, steel_top, steel_bottom)
        dc_x = columns(S, 0, speed_cols_in, n, 0, rs)
        dc_z = columns(S, 1, speed_cols_in, n, 1, rs)
        for h in range(nh):
            across, along = 0.5 * dr_x(h), 0.5 * dc_z(h)
            S[2, :, at(h)] = S[2, :, at(h)] + SC[1, :, at(h)] * across + SC[2, :, at(h)] * along
            S[3, :, at(h)] = S[3, :, at(h)] + SC[2, :, at(h)] * across + SC[3, :, at(h)] * along
            S[4, :, at(h)] = S[4, :, at(h)] + (0.5 * SC[4, :, at(h)]) * (dc_x(h) + dr_z(h))

    def water_speed(n):
        wait_rows(f"pr{n}", n, p_rows_in)
        wait_cols(f"pc{n}", n, p_cols_in)
        dr_p = rows_of(W, 0, p_rows_in, n, 0, water_top, water_bottom)
        dc_p = columns(W, 0, p_cols_in, n, None, rw)
        for h in range(nh):
            half = 0.5 * WC[0, :, at(h)]
            W[1, :, at(h)] = W[1, :, at(h)] - half * dr_p(h)
            W[2, :, at(h)] = W[2, :, at(h)] - half * dc_p(h)

    def water_pressure(n):
        wait_rows(f"vr{n}", n, vx_rows_in)
        wait_cols(f"vc{n}", n, vz_cols_in)
        dr_v = rows_of(W, 1, vx_rows_in, n, 0, water_top, water_bottom)
        dc_v = columns(W, 2, vz_cols_in, n, None, rw)
        for h in range(nh):
            W[0, :, at(h)] = W[0, :, at(h)] - (0.5 * WC[1, :, at(h)]) * (dr_v(h) + dc_v(h))

    def water_feed(values):
        fed = scatter(values * FAC[...], RW, LW)
        for h in range(nh):
            W[0, :, at(h)] = W[0, :, at(h)] + fed[h * rw : (h + 1) * rw, :]

    loads[4].wait()
    sample = gather(W.at[0], rw, RW, LW) * FAC[...]
    loads[6].wait()
    pl.semaphore_wait(barrier, sum(h.astype(jnp.int32) for h in has))

    send_stress(0)
    send_lists("s0", 0, sample)
    send_p(0)
    loads[5].wait()
    selectors(lane_row(steel_cell), rs, RS, LS)
    loads[7].wait()
    loads[8].wait()
    for n in range(STEPS):
        steel_speed(n)
        send_speed(n)
        water_speed(n)
        send_v(n)
        all_sent(f"sr{n}", (0, 1))
        all_sent(f"sc{n}", (2, 3))
        all_sent(f"pr{n}", (0, 1))
        all_sent(f"pc{n}", (2, 3))
        steel_load_values = receive_lists(f"s{n}", 2 * n, sample)
        all_sent(f"uc{n}", (2, 3))
        steel_load(steel_load_values)
        steel_stress(n)
        traction = gather(S.at[3], rs, RS, LS)
        send_lists(f"t{n}", 2 * n + 1, traction)
        if n < STEPS - 1:
            send_stress(n + 1)
        water_pressure(n)
        returning = receive_lists(f"t{n}", 2 * n + 1, traction)
        water_feed(returning)
        if n < STEPS - 1:
            sample = gather(W.at[0], rw, RW, LW) * FAC[...]
            send_lists(f"s{n + 1}", 2 * n + 2, sample)
            send_p(n + 1)
        all_sent(f"s{n}", (0, 1))
        all_sent(f"t{n}", (0, 1))
        all_sent(f"ur{n}", (0, 1))
        all_sent(f"vr{n}", (0, 1))
        all_sent(f"vc{n}", (2, 3))


def store_kernel(water, steel, water_out, steel_out, sem):
    stores = [
        pltpu.make_async_copy(steel, steel_out, sem.at[0]),
        pltpu.make_async_copy(water, water_out, sem.at[1]),
    ]
    for store in stores:
        store.start()
    for store in stores:
        store.wait()


def on_device(
    tiles,
    subs,
    water_state,
    water_coef,
    steel_state,
    steel_coef,
    coupling,
    water_cell,
    stencil_code,
    link_count,
    steel_cell,
):
    rw, nz = water_state.shape[1:]
    rs = steel_state.shape[1]
    cap = water_cell.shape[1]
    slots = 3 * cap
    nh = nz // LANES
    vmem = pl.BlockSpec(memory_space=pltpu.VMEM)
    hbm = pl.BlockSpec(memory_space=pltpu.HBM)
    rows_of = lambda fields: pltpu.VMEM((2, STEPS, fields, 1, nz), F32)
    results = pl.pallas_call(
        functools.partial(kernel, (tiles, subs, rw, rs, nz, cap)),
        out_shape=(
            pltpu.VMEM(water_state.shape, F32),
            pltpu.VMEM(steel_state.shape, F32),
        ),
        in_specs=[hbm] * 9,
        out_specs=(vmem, vmem),
        scratch_shapes=[
            pltpu.SMEM(coupling.shape, F32),
            pltpu.SMEM((1, 3), jnp.int32),
            pltpu.VMEM(water_cell.shape, jnp.int32),
            pltpu.VMEM(water_cell.shape, jnp.int32),
            pltpu.VMEM(water_cell.shape, jnp.int32),
            pltpu.VMEM(water_coef.shape, F32),
            pltpu.VMEM(steel_coef.shape, F32),
            pltpu.VMEM((nh * rw, slots), BF16),
            pltpu.VMEM((nh * rs, slots), BF16),
            pltpu.VMEM((LANES, slots), F32),
            pltpu.VMEM((LANES, slots), F32),
            pltpu.VMEM((1, slots), F32),
            pltpu.VMEM((nh * rs, LANES), F32),
            pltpu.VMEM((2, 2 * STEPS, 1, cap), F32),
            pltpu.VMEM((2, 2 * STEPS, 1, cap), F32),
            rows_of(2),
            rows_of(2),
            rows_of(2),
            rows_of(2),
            rows_of(1),
            rows_of(1),
            rows_of(1),
            rows_of(1),
            pltpu.VMEM((2, STEPS, 2, rs, LANES), F32),
            pltpu.VMEM((2, STEPS, 2, rs, LANES), F32),
            pltpu.VMEM((2, STEPS, rw, LANES), F32),
            pltpu.VMEM((2, STEPS, rw, LANES), F32),
            pltpu.SemaphoreType.DMA((9,)),
            pltpu.SemaphoreType.DMA((64,)),
            pltpu.SemaphoreType.DMA((64,)),
        ],
        compiler_params=pltpu.CompilerParams(
            collective_id=0, has_side_effects=True, vmem_limit_bytes=VMEM_BYTES - 4 * (water_state.size + steel_state.size)
        ),
    )(
        coupling,
        link_count.reshape(1, 3),
        water_cell,
        stencil_code,
        steel_cell,
        water_state,
        water_coef,
        steel_state,
        steel_coef,
    )
    return pl.pallas_call(
        store_kernel,
        out_shape=(
            jax.ShapeDtypeStruct(water_state.shape, F32),
            jax.ShapeDtypeStruct(steel_state.shape, F32),
        ),
        in_specs=[vmem, vmem],
        out_specs=(hbm, hbm),
        scratch_shapes=[pltpu.SemaphoreType.DMA((2,))],
        compiler_params=pltpu.CompilerParams(vmem_limit_bytes=1024 * 1024),
    )(*results)


def solution(mesh):
    in_specs = (
        P(None, "tile", "sub"),
        P(None, "tile", "sub"),
        P(None, "tile", "sub"),
        P(None, "tile", "sub"),
        P(),
        P("tile", "sub"),
        P("tile", "sub"),
        P("tile", "sub"),
        P("tile", "sub"),
    )
    out_specs = (P(None, "tile", "sub"), P(None, "tile", "sub"))
    return jax.shard_map(
        functools.partial(on_device, mesh.shape["tile"], mesh.shape["sub"]),
        mesh=mesh,
        in_specs=in_specs,
        out_specs=out_specs,
        check_vma=False,
    )
```

```python
import functools

import jax
import jax.numpy as jnp
from jax import lax
from jax.experimental import pallas as pl
from jax.experimental.pallas import tpu as pltpu
from jax.sharding import PartitionSpec as P

MESH = pl.DeviceIdType.MESH
STEPS = 3
LANES = 128
VMEM_BYTES = 67043328
F32 = jnp.float32
BF16 = jnp.bfloat16


def split_two(x):
    first = x.astype(BF16)
    return first, (x - first.astype(F32)).astype(BF16)


class Columns:
    def __init__(self, get, left, right, count, shape):
        self.get, self.left, self.right, self.count = get, left, right, count
        lane = lax.broadcasted_iota(jnp.int32, shape, 1)
        self.is_first, self.is_last = lane == 0, lane == LANES - 1
        self.before, self.after = {}, {}

    def tile(self, h):
        return self.left() if h < 0 else self.right() if h == self.count else self.get(h)

    def rolled(self, h, cache, shift):
        if h not in cache:
            cache[h] = pltpu.roll(self.tile(h), shift, 1)
        return cache[h]

    def __call__(self, h):
        previous = jnp.where(
            self.is_first, self.rolled(h - 1, self.before, 1), self.rolled(h, self.before, 1)
        )
        following = jnp.where(
            self.is_last,
            self.rolled(h + 1, self.after, LANES - 1),
            self.rolled(h, self.after, LANES - 1),
        )
        return following - previous


def row_difference(tile, above, below, is_top, is_bottom):
    rows = tile.shape[0]
    previous = jnp.where(is_top, above, pltpu.roll(tile, 1, 0))
    following = jnp.where(is_bottom, below, pltpu.roll(tile, rows - 1, 0))
    return following - previous


def kernel(
    dims,
    coupling_in,
    counts_in,
    water_cell_in,
    stencil_code_in,
    steel_cell_in,
    water_in,
    water_coef_in,
    steel_in,
    steel_coef_in,
    W,
    S,
    coupling,
    counts,
    water_cell,
    stencil_code,
    steel_cell,
    WC,
    SC,
    RW,
    RS,
    LW,
    LS,
    FAC,
    LOAD,
    lists_out,
    lists_in,
    stress_rows_out,
    stress_rows_in,
    speed_rows_out,
    speed_rows,
    p_rows_out,
    p_rows_in,
    vx_rows_out,
    vx_rows,
    stress_cols_in,
    speed_cols,
    p_cols_in,
    vz_cols,
    corners_in,
    local_sem,
    send_sem,
    recv_sem,
):
    tiles, subs, rw, rs, nz, cap = dims
    nh = nz // LANES
    shift = nz.bit_length() - 1
    slots = 3 * cap
    a = lax.axis_index("tile")
    c = lax.axis_index("sub")
    moves = ((-1, 0), (1, 0), (0, -1), (0, 1), (-1, -1), (-1, 1), (1, -1), (1, 1))
    opposite = (1, 0, 3, 2, 7, 6, 5, 4)
    along = {(0, -1): c > 0, (0, 1): c < subs - 1, (-1, 0): a > 0, (1, 0): a < tiles - 1}
    has = [
        along[m] if m in along else jnp.logical_and(along[(m[0], 0)], along[(0, m[1])])
        for m in moves
    ]
    target = [(a + m[0], c + m[1]) for m in moves]

    barrier = pltpu.get_barrier_semaphore()
    for d in range(8):

        @pl.when(has[d])
        def _():
            pl.semaphore_signal(barrier, inc=1, device_id=target[d], device_id_type=MESH)

    loads = [
        pltpu.make_async_copy(src, dst, local_sem.at[i])
        for i, (src, dst) in enumerate(
            (
                (coupling_in, coupling),
                (counts_in, counts),
                (stencil_code_in, stencil_code),
                (water_cell_in, water_cell),
                (water_in, W),
                (steel_cell_in, steel_cell),
                (steel_in, S),
                (water_coef_in, WC),
                (steel_coef_in, SC),
            )
        )
    ]
    for load in loads:
        load.start()

    ids = {}

    def copy(name, d, src, dst):
        key = (name, d)
        if key not in ids:
            ids[key] = len(ids)
        return pltpu.make_async_remote_copy(
            src_ref=src,
            dst_ref=dst,
            send_sem=send_sem.at[ids[key]],
            recv_sem=recv_sem.at[ids[key]],
            device_id=target[d],
            device_id_type=MESH,
        )

    pending = {}

    def send(name, d, src, dst):
        @pl.when(has[d])
        def _():
            copy(name, d, src, dst).start()

        pending[(name, d)] = (src, dst)

    def arrived(name, d, dst):
        @pl.when(has[opposite[d]])
        def _():
            copy(name, d, dst, dst).wait_recv()

    def sent(name, d):
        src, dst = pending.pop((name, d))

        @pl.when(has[d])
        def _():
            copy(name, d, src, dst).wait_send()

    row_refs = (lists_in, stress_rows_in, speed_rows, p_rows_in, vx_rows)
    col_refs = (stress_cols_in, speed_cols, p_cols_in, vz_cols)
    for d in range(8):

        @pl.when(jnp.logical_not(has[opposite[d]]))
        def _():
            for ref in row_refs if d < 2 else col_refs if d < 4 else (corners_in,):
                part = ref.at[d if d < 2 else d - 2 if d < 4 else d - 4]
                part[...] = jnp.zeros(part.shape, F32)

    for load in loads[:4]:
        load.wait()
    lane_row = lambda ref: jnp.concatenate([ref[0:1, :], ref[1:2, :], ref[2:3, :]], axis=1)
    wcell = lane_row(water_cell)
    code = lane_row(stencil_code)
    slot = lax.broadcasted_iota(jnp.int32, (1, cap), 1)
    live = jnp.concatenate([slot < counts[0, m] for m in range(3)], axis=1)
    weight = jnp.zeros((1, slots), F32)
    for k in range(9):
        weight = jnp.where(code == k, coupling[k], weight)
    FAC[...] = jnp.where(live, weight, 0.0)

    def selectors(cell, rows, R, L):
        row = cell >> shift
        key = ((cell >> 7) & (nh - 1)) * rows + row
        low = cell & (LANES - 1)
        count = nh * rows
        block = min(128, count)
        for k0 in range(0, count, block):
            index = lax.broadcasted_iota(jnp.int32, (block, slots), 0) + k0
            R[k0 : k0 + block, :] = jnp.where(index == key, 1.0, 0.0).astype(BF16)
        index = lax.broadcasted_iota(jnp.int32, (LANES, slots), 0)
        L[...] = jnp.where(index == low, 1.0, 0.0)

    selectors(wcell, rw, RW, LW)

    def gather(field, rows, R, L):
        stacked = jnp.concatenate(
            [field[:, h * LANES : (h + 1) * LANES] for h in range(nh)], axis=0
        )
        parts = split_two(jnp.transpose(stacked))
        picked = jnp.dot(
            jnp.concatenate(parts, axis=0), R[...], preferred_element_type=F32
        )
        picked = (picked[:LANES] + picked[LANES:]) * L[...]
        return jnp.sum(picked, axis=0, keepdims=True)

    def scatter(values, R, L):
        parts = split_two(L[...] * values)
        spread = lax.dot_general(
            R[...],
            jnp.concatenate(parts, axis=0),
            (((1,), (1,)), ((), ())),
            preferred_element_type=F32,
        )
        return spread[:, :LANES] + spread[:, LANES:]

    def masks(rows):
        row = lax.broadcasted_iota(jnp.int32, (rows, LANES), 0)
        return row == 0, row == rows - 1

    steel_top, steel_bottom = masks(rs)
    water_top, water_bottom = masks(rw)
    at = lambda h: slice(h * LANES, (h + 1) * LANES)

    def send_lists(name, n, values):
        lists_out[0, n] = values[:, :cap]
        lists_out[1, n] = values[:, 2 * cap :]
        for d in (0, 1):
            send(name, d, lists_out.at[d, n], lists_in.at[d, n])

    def receive_lists(name, n, values):
        for d in (0, 1):
            arrived(name, d, lists_in.at[d, n])
        return jnp.concatenate(
            [lists_in[1, n], values[:, cap : 2 * cap], lists_in[0, n]], axis=1
        )

    first, last = slice(0, LANES), slice(nz - LANES, nz)
    stress_rows = ((2, 0), (4, 0), (3, 0), (2, 1), (4, 1))

    def put_row(out, ref, f, r):
        for h in range(nh):
            out[h : h + 1, :] = ref[f, r : r + 1, at(h)]

    def send_stress(n):
        for d in (0, 1):
            for i, (f, r) in enumerate(stress_rows):
                put_row(stress_rows_out.at[d, n, i], S, f, rs - 1 - r if d else r)
            send(f"sr{n}", d, stress_rows_out.at[d, n], stress_rows_in.at[d, n])
        for d, lanes in ((2, first), (3, last)):
            send(f"sc{n}", d, S.at[2:5, :, lanes], stress_cols_in.at[d - 2, n])
        for d in range(4, 8):
            rows = slice(0, 8) if moves[d][0] < 0 else slice(rs - 8, rs)
            lanes = first if moves[d][1] < 0 else last
            send(f"sd{n}", d, S.at[2:5, rows, lanes], corners_in.at[d - 4, n])

    def send_speed():
        for d in (0, 1):
            for i, (ref, f) in enumerate(((S, 0), (S, 1), (SC, 0))):
                put_row(speed_rows_out.at[d, i], ref, f, rs - 1 if d else 0)
            send("ur", d, speed_rows_out.at[d], speed_rows.at[d])
        for d, lanes in ((2, first), (3, last)):
            send("uc", d, S.at[0:2, :, lanes], speed_cols.at[d - 2, 0:2])
            send("bc", d, SC.at[0:1, :, lanes], speed_cols.at[d - 2, 2:3])

    def send_p(n):
        for d in (0, 1):
            for r in (0, 1):
                put_row(p_rows_out.at[d, n, r], W, 0, rw - 1 - r if d else r)
            send(f"pr{n}", d, p_rows_out.at[d, n], p_rows_in.at[d, n])
        for d, lanes in ((2, first), (3, last)):
            send(f"pc{n}", d, W.at[0, :, lanes], p_cols_in.at[d - 2, n])

    def send_v():
        for d in (0, 1):
            for i, (ref, f) in enumerate(((W, 1), (WC, 0))):
                put_row(vx_rows_out.at[d, i], ref, f, rw - 1 if d else 0)
            send("vr", d, vx_rows_out.at[d], vx_rows.at[d])
        for d, lanes in ((2, first), (3, last)):
            send("vc", d, W.at[2:3, :, lanes], vz_cols.at[d - 2, 0:1])
            send("wc", d, WC.at[0:1, :, lanes], vz_cols.at[d - 2, 1:2])

    def wait_stress(n):
        for d in (0, 1):
            arrived(f"sr{n}", d, stress_rows_in.at[d, n])
        for d in (2, 3):
            arrived(f"sc{n}", d, stress_cols_in.at[d - 2, n])
        for d in range(4, 8):
            arrived(f"sd{n}", d, corners_in.at[d - 4, n])

    def wait_speed():
        for d in (0, 1):
            arrived("ur", d, speed_rows.at[d])
        for d in (2, 3):
            arrived("uc", d, speed_cols.at[d - 2, 0:2])
            arrived("bc", d, speed_cols.at[d - 2, 2:3])

    def wait_p(n):
        for d in (0, 1):
            arrived(f"pr{n}", d, p_rows_in.at[d, n])
        for d in (2, 3):
            arrived(f"pc{n}", d, p_cols_in.at[d - 2, n])

    def wait_v():
        for d in (0, 1):
            arrived("vr", d, vx_rows.at[d])
        for d in (2, 3):
            arrived("vc", d, vz_cols.at[d - 2, 0:1])
            arrived("wc", d, vz_cols.at[d - 2, 1:2])

    def all_sent(name, directions):
        for d in directions:
            sent(name, d)

    def columns(ref, f, into, rows):
        return Columns(
            lambda h: ref[f, :, at(h)], lambda: into(1), lambda: into(0), nh, (rows, LANES)
        )

    def rows_of(ref, f, into, top, bottom):
        return lambda h: row_difference(
            ref[f, :, at(h)], into(1)[h : h + 1, :], into(0)[h : h + 1, :], top, bottom
        )

    line = lax.broadcasted_iota(jnp.int32, (nh, LANES), 0)
    lane = lax.broadcasted_iota(jnp.int32, (nh, LANES), 1)

    def along_row(x, left, right):
        before, after = pltpu.roll(x, 1, 1), pltpu.roll(x, LANES - 1, 1)
        wrapped = jnp.where(line == 0, pltpu.roll(left, 1, 1), pltpu.roll(before, 1, 0))
        previous = jnp.where(lane == 0, wrapped, before)
        wrapped = jnp.where(
            line == nh - 1, pltpu.roll(right, LANES - 1, 1), pltpu.roll(after, nh - 1, 0)
        )
        return jnp.where(lane == LANES - 1, wrapped, after) - previous

    def beside(side, tile, ref, f):
        if side:
            return pltpu.roll(ref[f, :, first], LANES - 1, 1) - pltpu.roll(tile, 1, 1)
        return pltpu.roll(tile, LANES - 1, 1) - pltpu.roll(ref[f, :, last], 1, 1)

    def corner(up, left, n, i):
        r = 7 if up else 0
        return corners_in[2 * up + left, n, i, r : r + 1, :]

    def outer_speed(n):
        for side in (1, 0):
            near = stress_rows_out[1 - side, n]
            far = stress_rows_in[side, n]
            half = 0.5 * speed_rows[side, 2]
            for i, (own, beyond, flat, field) in enumerate(((0, 3, 1, 2), (1, 4, 2, 1))):
                across = near[own] - far[beyond] if side else far[beyond] - near[own]
                change = along_row(far[flat], corner(side, 1, n, field), corner(side, 0, n, field))
                speed_rows[side, i] = speed_rows[side, i] + half * (across + change)
        for side in (1, 0):
            half = 0.5 * speed_cols[side, 2]
            for i, (down, flat) in enumerate(((0, 2), (2, 1))):
                across = row_difference(
                    stress_cols_in[side, n, down],
                    corner(1, side, n, down),
                    corner(0, side, n, down),
                    steel_top,
                    steel_bottom,
                )
                change = beside(side, stress_cols_in[side, n, flat], S, flat + 2)
                speed_cols[side, i] = speed_cols[side, i] + half * (across + change)

    def steel_speed(n):
        rows_in = lambda i: lambda side: stress_rows_in.at[side, n, i]
        cols_in = lambda i: lambda side: stress_cols_in[side, n, i]
        dr_xx = rows_of(S, 2, rows_in(0), steel_top, steel_bottom)
        dr_xz = rows_of(S, 4, rows_in(1), steel_top, steel_bottom)
        dc_zz = columns(S, 3, cols_in(1), rs)
        dc_xz = columns(S, 4, cols_in(2), rs)
        for h in range(nh):
            half = 0.5 * SC[0, :, at(h)]
            S[0, :, at(h)] = S[0, :, at(h)] + half * (dr_xx(h) + dc_xz(h))
            S[1, :, at(h)] = S[1, :, at(h)] + half * (dr_xz(h) + dc_zz(h))

    def steel_load(values):
        LOAD[...] = scatter(values, RS, LS)
        for h in range(nh):
            S[1, :, at(h)] = S[1, :, at(h)] - SC[0, :, at(h)] * LOAD[h * rs : (h + 1) * rs, :]

    def steel_stress():
        rows_in = lambda i: lambda side: speed_rows.at[side, i]
        cols_in = lambda i: lambda side: speed_cols[side, i]
        dr_x = rows_of(S, 0, rows_in(0), steel_top, steel_bottom)
        dr_z = rows_of(S, 1, rows_in(1), steel_top, steel_bottom)
        dc_x = columns(S, 0, cols_in(0), rs)
        dc_z = columns(S, 1, cols_in(1), rs)
        for h in range(nh):
            across, along = 0.5 * dr_x(h), 0.5 * dc_z(h)
            S[2, :, at(h)] = S[2, :, at(h)] + SC[1, :, at(h)] * across + SC[2, :, at(h)] * along
            S[3, :, at(h)] = S[3, :, at(h)] + SC[2, :, at(h)] * across + SC[3, :, at(h)] * along
            S[4, :, at(h)] = S[4, :, at(h)] + (0.5 * SC[4, :, at(h)]) * (dc_x(h) + dr_z(h))

    def water_speed(n):
        for side in (1, 0):
            near, far = p_rows_out[1 - side, n, 0], p_rows_in[side, n, 1]
            across = near - far if side else far - near
            vx_rows[side, 0] = vx_rows[side, 0] - (0.5 * vx_rows[side, 1]) * across
            change = beside(side, p_cols_in[side, n], W, 0)
            vz_cols[side, 0] = vz_cols[side, 0] - (0.5 * vz_cols[side, 1]) * change
        dr_p = rows_of(W, 0, lambda side: p_rows_in.at[side, n, 0], water_top, water_bottom)
        dc_p = columns(W, 0, lambda side: p_cols_in[side, n], rw)
        for h in range(nh):
            half = 0.5 * WC[0, :, at(h)]
            W[1, :, at(h)] = W[1, :, at(h)] - half * dr_p(h)
            W[2, :, at(h)] = W[2, :, at(h)] - half * dc_p(h)

    def water_pressure():
        dr_v = rows_of(W, 1, lambda side: vx_rows.at[side, 0], water_top, water_bottom)
        dc_v = columns(W, 2, lambda side: vz_cols[side, 0], rw)
        for h in range(nh):
            W[0, :, at(h)] = W[0, :, at(h)] - (0.5 * WC[1, :, at(h)]) * (dr_v(h) + dc_v(h))

    def water_feed(values):
        fed = scatter(values * FAC[...], RW, LW)
        for h in range(nh):
            W[0, :, at(h)] = W[0, :, at(h)] + fed[h * rw : (h + 1) * rw, :]

    loads[4].wait()
    sample = gather(W.at[0], rw, RW, LW) * FAC[...]
    loads[6].wait()
    pl.semaphore_wait(barrier, sum(h.astype(jnp.int32) for h in has))
    send_lists("s0", 0, sample)
    send_stress(0)
    loads[8].wait()
    send_speed()
    loads[7].wait()
    send_p(0)
    send_v()
    loads[5].wait()
    selectors(lane_row(steel_cell), rs, RS, LS)
    for n in range(STEPS):
        wait_stress(n)
        if n == 0:
            wait_speed()
            all_sent("uc", (2, 3))
        outer_speed(n)
        steel_speed(n)
        loading = receive_lists(f"s{n}", 2 * n, sample)
        all_sent(f"sc{n}", (2, 3))
        all_sent(f"sd{n}", range(4, 8))
        steel_load(loading)
        steel_stress()
        traction = gather(S.at[3], rs, RS, LS)
        send_lists(f"t{n}", 2 * n + 1, traction)
        if n < STEPS - 1:
            send_stress(n + 1)
        wait_p(n)
        if n == 0:
            wait_v()
            all_sent("vc", (2, 3))
        water_speed(n)
        all_sent(f"pc{n}", (2, 3))
        water_pressure()
        returning = receive_lists(f"t{n}", 2 * n + 1, traction)
        water_feed(returning)
        if n < STEPS - 1:
            sample = gather(W.at[0], rw, RW, LW) * FAC[...]
            send_lists(f"s{n + 1}", 2 * n + 2, sample)
            send_p(n + 1)
    for name, d in list(pending):
        sent(name, d)


def store_kernel(water, steel, water_out, steel_out, sem):
    stores = [
        pltpu.make_async_copy(steel, steel_out, sem.at[0]),
        pltpu.make_async_copy(water, water_out, sem.at[1]),
    ]
    for store in stores:
        store.start()
    for store in stores:
        store.wait()


def on_device(
    tiles,
    subs,
    water_state,
    water_coef,
    steel_state,
    steel_coef,
    coupling,
    water_cell,
    stencil_code,
    link_count,
    steel_cell,
):
    rw, nz = water_state.shape[1:]
    rs = steel_state.shape[1]
    cap = water_cell.shape[1]
    slots = 3 * cap
    nh = nz // LANES
    vmem = pl.BlockSpec(memory_space=pltpu.VMEM)
    hbm = pl.BlockSpec(memory_space=pltpu.HBM)
    rows_of = lambda *lead: pltpu.VMEM((2, *lead, nh, LANES), F32)
    results = pl.pallas_call(
        functools.partial(kernel, (tiles, subs, rw, rs, nz, cap)),
        out_shape=(
            pltpu.VMEM(water_state.shape, F32),
            pltpu.VMEM(steel_state.shape, F32),
        ),
        in_specs=[hbm] * 9,
        out_specs=(vmem, vmem),
        scratch_shapes=[
            pltpu.SMEM(coupling.shape, F32),
            pltpu.SMEM((1, 3), jnp.int32),
            pltpu.VMEM(water_cell.shape, jnp.int32),
            pltpu.VMEM(water_cell.shape, jnp.int32),
            pltpu.VMEM(water_cell.shape, jnp.int32),
            pltpu.VMEM(water_coef.shape, F32),
            pltpu.VMEM(steel_coef.shape, F32),
            pltpu.VMEM((nh * rw, slots), BF16),
            pltpu.VMEM((nh * rs, slots), BF16),
            pltpu.VMEM((LANES, slots), F32),
            pltpu.VMEM((LANES, slots), F32),
            pltpu.VMEM((1, slots), F32),
            pltpu.VMEM((nh * rs, LANES), F32),
            pltpu.VMEM((2, 2 * STEPS, 1, cap), F32),
            pltpu.VMEM((2, 2 * STEPS, 1, cap), F32),
            rows_of(STEPS, 5),
            rows_of(STEPS, 5),
            rows_of(3),
            rows_of(3),
            rows_of(STEPS, 2),
            rows_of(STEPS, 2),
            rows_of(2),
            rows_of(2),
            pltpu.VMEM((2, STEPS, 3, rs, LANES), F32),
            pltpu.VMEM((2, 3, rs, LANES), F32),
            pltpu.VMEM((2, STEPS, rw, LANES), F32),
            pltpu.VMEM((2, 2, rw, LANES), F32),
            pltpu.VMEM((4, STEPS, 3, 8, LANES), F32),
            pltpu.SemaphoreType.DMA((9,)),
            pltpu.SemaphoreType.DMA((80,)),
            pltpu.SemaphoreType.DMA((80,)),
        ],
        compiler_params=pltpu.CompilerParams(
            collective_id=0, has_side_effects=True, vmem_limit_bytes=VMEM_BYTES - 4 * (water_state.size + steel_state.size)
        ),
    )(
        coupling,
        link_count.reshape(1, 3),
        water_cell,
        stencil_code,
        steel_cell,
        water_state,
        water_coef,
        steel_state,
        steel_coef,
    )
    return pl.pallas_call(
        store_kernel,
        out_shape=(
            jax.ShapeDtypeStruct(water_state.shape, F32),
            jax.ShapeDtypeStruct(steel_state.shape, F32),
        ),
        in_specs=[vmem, vmem],
        out_specs=(hbm, hbm),
        scratch_shapes=[pltpu.SemaphoreType.DMA((2,))],
        compiler_params=pltpu.CompilerParams(vmem_limit_bytes=1024 * 1024),
    )(*results)


def solution(mesh):
    in_specs = (
        P(None, "tile", "sub"),
        P(None, "tile", "sub"),
        P(None, "tile", "sub"),
        P(None, "tile", "sub"),
        P(),
        P("tile", "sub"),
        P("tile", "sub"),
        P("tile", "sub"),
        P("tile", "sub"),
    )
    out_specs = (P(None, "tile", "sub"), P(None, "tile", "sub"))
    return jax.shard_map(
        functools.partial(on_device, mesh.shape["tile"], mesh.shape["sub"]),
        mesh=mesh,
        in_specs=in_specs,
        out_specs=out_specs,
        check_vma=False,
    )
```

```python
import functools

import jax
import jax.numpy as jnp
from jax import lax
from jax.experimental import pallas as pl
from jax.experimental.pallas import tpu as pltpu
from jax.sharding import PartitionSpec as P

MESH = pl.DeviceIdType.MESH
STEPS = 3
LANES = 128
VMEM_BYTES = 67043328
F32 = jnp.float32
BF16 = jnp.bfloat16


def split_two(x):
    first = x.astype(BF16)
    return first, (x - first.astype(F32)).astype(BF16)


class Columns:
    def __init__(self, get, left, right, count, shape):
        self.get, self.left, self.right, self.count = get, left, right, count
        lane = lax.broadcasted_iota(jnp.int32, shape, 1)
        self.is_first, self.is_last = lane == 0, lane == LANES - 1
        self.before, self.after = {}, {}

    def tile(self, h):
        return self.left() if h < 0 else self.right() if h == self.count else self.get(h)

    def rolled(self, h, cache, shift):
        if h not in cache:
            cache[h] = pltpu.roll(self.tile(h), shift, 1)
        return cache[h]

    def __call__(self, h):
        previous = jnp.where(
            self.is_first, self.rolled(h - 1, self.before, 1), self.rolled(h, self.before, 1)
        )
        following = jnp.where(
            self.is_last,
            self.rolled(h + 1, self.after, LANES - 1),
            self.rolled(h, self.after, LANES - 1),
        )
        return following - previous


def row_difference(tile, above, below, is_top, is_bottom):
    rows = tile.shape[0]
    previous = jnp.where(is_top, above, pltpu.roll(tile, 1, 0))
    following = jnp.where(is_bottom, below, pltpu.roll(tile, rows - 1, 0))
    return following - previous


def kernel(
    dims,
    coupling_in,
    counts_in,
    water_cell_in,
    stencil_code_in,
    steel_cell_in,
    water_in,
    water_coef_in,
    steel_in,
    steel_coef_in,
    W,
    S,
    coupling,
    counts,
    water_cell,
    stencil_code,
    steel_cell,
    WC,
    SC,
    RW,
    RS,
    LW,
    LS,
    FAC,
    LOAD,
    EQ,
    lists_out,
    lists_in,
    near_out,
    near_in,
    far_out,
    far_in,
    known_out,
    known_in,
    stress_rows_out,
    stress_rows_in,
    part_rows_out,
    part_rows_in,
    coef_rows_out,
    coef_rows_in,
    speed_rows,
    p_rows_out,
    p_rows_in,
    wcoef_rows_out,
    wcoef_rows_in,
    vx_rows,
    stress_cols_in,
    part_cols_in,
    coef_cols_in,
    speed_cols,
    p_cols_in,
    vz_cols_in,
    wcoef_cols_in,
    vz_cols,
    corners_in,
    local_sem,
    send_sem,
    recv_sem,
):
    tiles, subs, rw, rs, nz, cap = dims
    nh = nz // LANES
    shift = nz.bit_length() - 1
    slots = 3 * cap
    a = lax.axis_index("tile")
    c = lax.axis_index("sub")
    moves = ((-1, 0), (1, 0), (0, -1), (0, 1), (-1, -1), (-1, 1), (1, -1), (1, 1), (-2, 0), (2, 0))
    opposite = (1, 0, 3, 2, 7, 6, 5, 4, 9, 8)
    along = {
        (0, -1): c > 0,
        (0, 1): c < subs - 1,
        (-1, 0): a > 0,
        (1, 0): a < tiles - 1,
        (-2, 0): a > 1,
        (2, 0): a < tiles - 2,
    }
    has = [
        along[m] if m in along else jnp.logical_and(along[(m[0], 0)], along[(0, m[1])])
        for m in moves
    ]
    target = [(a + m[0], c + m[1]) for m in moves]

    barrier = pltpu.get_barrier_semaphore()
    for d in range(10):

        @pl.when(has[d])
        def _():
            pl.semaphore_signal(barrier, inc=1, device_id=target[d], device_id_type=MESH)

    loads = [
        pltpu.make_async_copy(src, dst, local_sem.at[i])
        for i, (src, dst) in enumerate(
            (
                (coupling_in, coupling),
                (counts_in, counts),
                (stencil_code_in, stencil_code),
                (water_cell_in, water_cell),
                (water_in, W),
                (steel_cell_in, steel_cell),
                (steel_in, S),
                (water_coef_in, WC),
                (steel_coef_in, SC),
            )
        )
    ]
    for load in loads:
        load.start()

    ids = {}

    def copy(name, d, src, dst):
        key = (name, d)
        if key not in ids:
            ids[key] = len(ids)
        return pltpu.make_async_remote_copy(
            src_ref=src,
            dst_ref=dst,
            send_sem=send_sem.at[ids[key]],
            recv_sem=recv_sem.at[ids[key]],
            device_id=target[d],
            device_id_type=MESH,
        )

    pending = {}

    def send(name, d, src, dst):
        @pl.when(has[d])
        def _():
            copy(name, d, src, dst).start()

        pending[(name, d)] = (src, dst)

    def arrived(name, d, dst):
        @pl.when(has[opposite[d]])
        def _():
            copy(name, d, dst, dst).wait_recv()

    def sent(name, d):
        src, dst = pending.pop((name, d))

        @pl.when(has[d])
        def _():
            copy(name, d, src, dst).wait_send()

    row_refs = (
        lists_in,
        near_in,
        known_in,
        stress_rows_in,
        part_rows_in,
        coef_rows_in,
        p_rows_in,
        wcoef_rows_in,
    )
    col_refs = (
        stress_cols_in,
        part_cols_in,
        coef_cols_in,
        p_cols_in,
        vz_cols_in,
        wcoef_cols_in,
    )
    for d in range(10):
        refs = row_refs if d < 2 else col_refs if d < 4 else (corners_in,) if d < 8 else (far_in,)

        @pl.when(jnp.logical_not(has[opposite[d]]))
        def _():
            for ref in refs:
                part = ref.at[d if d < 2 else d - 2 if d < 4 else d - 4 if d < 8 else d - 8]
                part[...] = jnp.zeros(part.shape, F32)

    for load in loads[:4]:
        load.wait()
    lane_row = lambda ref: jnp.concatenate([ref[0:1, :], ref[1:2, :], ref[2:3, :]], axis=1)
    wcell = lane_row(water_cell)
    code = lane_row(stencil_code)
    slot = lax.broadcasted_iota(jnp.int32, (1, cap), 1)
    live = jnp.concatenate([slot < counts[0, m] for m in range(3)], axis=1)
    weight = jnp.zeros((1, slots), F32)
    for k in range(9):
        weight = jnp.where(code == k, coupling[k], weight)
    FAC[...] = jnp.where(live, weight, 0.0)

    def selectors(cell, rows, R, L):
        row = cell >> shift
        key = ((cell >> 7) & (nh - 1)) * rows + row
        low = cell & (LANES - 1)
        count = nh * rows
        block = min(128, count)
        for k0 in range(0, count, block):
            index = lax.broadcasted_iota(jnp.int32, (block, slots), 0) + k0
            R[k0 : k0 + block, :] = jnp.where(index == key, 1.0, 0.0).astype(BF16)
        index = lax.broadcasted_iota(jnp.int32, (LANES, slots), 0)
        L[...] = jnp.where(index == low, 1.0, 0.0)

    selectors(wcell, rw, RW, LW)

    def gather(field, rows, R, L):
        stacked = jnp.concatenate(
            [field[:, h * LANES : (h + 1) * LANES] for h in range(nh)], axis=0
        )
        parts = split_two(jnp.transpose(stacked))
        picked = jnp.dot(
            jnp.concatenate(parts, axis=0), R[...], preferred_element_type=F32
        )
        picked = (picked[:LANES] + picked[LANES:]) * L[...]
        return jnp.sum(picked, axis=0, keepdims=True)

    def scatter(values, R, L):
        parts = split_two(L[...] * values)
        spread = lax.dot_general(
            R[...],
            jnp.concatenate(parts, axis=0),
            (((1,), (1,)), ((), ())),
            preferred_element_type=F32,
        )
        return spread[:, :LANES] + spread[:, LANES:]

    def masks(rows):
        row = lax.broadcasted_iota(jnp.int32, (rows, LANES), 0)
        return row == 0, row == rows - 1

    steel_top, steel_bottom = masks(rs)
    water_top, water_bottom = masks(rw)
    at = lambda h: slice(h * LANES, (h + 1) * LANES)

    def send_lists(name, n, values):
        lists_out[0, n] = values[:, :cap]
        lists_out[1, n] = values[:, 2 * cap :]
        for d in (0, 1):
            send(name, d, lists_out.at[d, n], lists_in.at[d, n])

    def wait_lists(name, n):
        for d in (0, 1):
            arrived(name, d, lists_in.at[d, n])

    def send_tractions(n, values):
        near_out[0, n] = values[:, : 2 * cap]
        near_out[1, n] = values[:, cap:]
        for d in (0, 1):
            send(f"t{n}", d, near_out.at[d, n], near_in.at[d, n])
        if n < STEPS - 1:
            far_out[0, n] = values[:, :cap]
            far_out[1, n] = values[:, 2 * cap :]
            for d in (8, 9):
                send(f"f{n}", d, far_out.at[d - 8, n], far_in.at[d - 8, n])

    def wait_tractions(n):
        for d in (0, 1):
            arrived(f"t{n}", d, near_in.at[d, n])
        if n < STEPS - 1:
            for d in (8, 9):
                arrived(f"f{n}", d, far_in.at[d - 8, n])

    first, last = slice(0, LANES), slice(nz - LANES, nz)

    def put_row(out, ref, f, r):
        for h in range(nh):
            out[h : h + 1, :] = ref[f, r : r + 1, at(h)]

    def put_rows(out, fields, rows):
        for d in (0, 1):
            for i, (ref, f) in enumerate(fields):
                put_row(out(d).at[i], ref, f, rows - 1 if d else 0)

    put_stress = lambda n: put_rows(lambda d: stress_rows_out.at[d, n], ((S, 2), (S, 4)), rs)
    put_part = lambda n: put_rows(lambda d: part_rows_out.at[d, n], ((S, 0), (S, 1)), rs)
    put_p = lambda n: put_rows(lambda d: p_rows_out.at[d, n, 0:1], ((W, 0),), rw)
    put_vx = lambda n: put_rows(lambda d: p_rows_out.at[d, n, 1:2], ((W, 1),), rw)

    edges = ((2, first), (3, last))
    all_rows = lambda name, out, into: [send(name, d, out(d), into(d)) for d in (0, 1)]
    all_cols = lambda name, src, into: [
        send(name, d, src(lanes), into(d - 2)) for d, lanes in edges
    ]

    def send_stress(n):
        all_rows(f"sr{n}", lambda d: stress_rows_out.at[d, n], lambda d: stress_rows_in.at[d, n])
        all_cols(f"sc{n}", lambda e: S.at[3:5, :, e], lambda d: stress_cols_in.at[d, n])
        for d in range(4, 8):
            rows = slice(0, 8) if moves[d][0] < 0 else slice(rs - 8, rs)
            lanes = first if moves[d][1] < 0 else last
            send(f"sd{n}", d, S.at[2:5, rows, lanes], corners_in.at[d - 4, n])

    def send_part(n):
        all_rows(f"ar{n}", lambda d: part_rows_out.at[d, n], lambda d: part_rows_in.at[d, n])
        all_cols(f"uc{n}", lambda e: S.at[0:2, :, e], lambda d: part_cols_in.at[d, n])

    def send_p(n):
        all_rows(f"pr{n}", lambda d: p_rows_out.at[d, n], lambda d: p_rows_in.at[d, n])
        all_cols(f"pc{n}", lambda e: W.at[0:1, :, e], lambda d: p_cols_in.at[d, n])
        all_cols(f"vc{n}", lambda e: W.at[2:3, :, e], lambda d: vz_cols_in.at[d, n])

    def wait_steel(n):
        for d in (0, 1):
            arrived(f"sr{n}", d, stress_rows_in.at[d, n])
        for d in (2, 3):
            arrived(f"sc{n}", d, stress_cols_in.at[d - 2, n])
        for d in range(4, 8):
            arrived(f"sd{n}", d, corners_in.at[d - 4, n])
        for d in (0, 1):
            arrived(f"ar{n}", d, part_rows_in.at[d, n])
        for d in (2, 3):
            arrived(f"uc{n}", d, part_cols_in.at[d - 2, n])

    def wait_water(n):
        for d in (0, 1):
            arrived(f"pr{n}", d, p_rows_in.at[d, n])
        for d in (2, 3):
            arrived(f"pc{n}", d, p_cols_in.at[d - 2, n])
            arrived(f"vc{n}", d, vz_cols_in.at[d - 2, n])

    def all_sent(name, directions):
        for d in directions:
            sent(name, d)

    def columns(ref, f, rows, into=None):
        zero = jnp.zeros((rows, LANES), F32)
        side = (lambda s: zero) if into is None else into
        return Columns(lambda h: ref[f, :, at(h)], lambda: side(1), lambda: side(0), nh, (rows, LANES))

    def rows_of(ref, f, top, bottom, into=None):
        side = lambda s, h: 0.0 if into is None else into(s)[h : h + 1, :]
        return lambda h: row_difference(ref[f, :, at(h)], side(1, h), side(0, h), top, bottom)

    line = lax.broadcasted_iota(jnp.int32, (nh, LANES), 0)
    lane = lax.broadcasted_iota(jnp.int32, (nh, LANES), 1)
    row_start = jnp.logical_and(line == 0, lane == 0)
    row_end = jnp.logical_and(line == nh - 1, lane == LANES - 1)

    def lanes_of(rows):
        index = lax.broadcasted_iota(jnp.int32, (rows, LANES), 1)
        return index == 0, index == LANES - 1

    back = lambda x: pltpu.roll(x, 1, 1)
    forth = lambda x: pltpu.roll(x, LANES - 1, 1)

    def outside_rows(above, below, top, bottom):
        return jnp.where(top, -above, jnp.where(bottom, below, 0.0))

    def outside_cols(h, rows, left, right):
        start, end = lanes_of(rows)
        if h == 0:
            return jnp.where(start, -back(left), 0.0)
        if h == nh - 1:
            return jnp.where(end, forth(right), 0.0)
        return None

    def corner(up, left, n, i):
        r = 7 if up else 0
        return corners_in[2 * up + left, n, i, r : r + 1, :]

    def outer_speed(n):
        for side in (1, 0):
            half = 0.5 * coef_rows_in[side, 0]
            for i, field in ((0, 2), (1, 1)):
                near = stress_rows_out[1 - side, n, i]
                change = jnp.where(row_end, forth(corner(side, 0, n, field)), 0.0) - jnp.where(
                    row_start, back(corner(side, 1, n, field)), 0.0
                )
                change = change + near if side else change - near
                speed_rows[side, i] = part_rows_in[side, n, i] + half * change
        for side in (1, 0):
            half = 0.5 * coef_cols_in[side, 0]
            for i, (down, flat) in enumerate(((0, 4), (2, 3))):
                change = outside_rows(
                    corner(1, side, n, down), corner(0, side, n, down), steel_top, steel_bottom
                )
                if side:
                    change = change + forth(S[flat, :, first])
                else:
                    change = change - back(S[flat, :, last])
                speed_cols[side, i] = part_cols_in[side, n, i] + half * change

    def steel_part():
        dr_xx = rows_of(S, 2, steel_top, steel_bottom)
        dr_xz = rows_of(S, 4, steel_top, steel_bottom)
        dc_zz = columns(S, 3, rs)
        dc_xz = columns(S, 4, rs)
        for h in range(nh):
            half = 0.5 * SC[0, :, at(h)]
            S[0, :, at(h)] = S[0, :, at(h)] + half * (dr_xx(h) + dc_xz(h))
            S[1, :, at(h)] = S[1, :, at(h)] + half * (dr_xz(h) + dc_zz(h))

    def steel_rest(n):
        for h in range(nh):
            half = 0.5 * SC[0, :, at(h)]
            changes = []
            for i, flat in ((0, 1), (1, 0)):
                change = outside_rows(
                    stress_rows_in[1, n, i, h : h + 1, :],
                    stress_rows_in[0, n, i, h : h + 1, :],
                    steel_top,
                    steel_bottom,
                )
                if h in (0, nh - 1):
                    change = change + outside_cols(
                        h, rs, stress_cols_in[1, n, flat], stress_cols_in[0, n, flat]
                    )
                changes.append(change)
            S[0, :, at(h)] = S[0, :, at(h)] + half * changes[0]
            S[1, :, at(h)] = S[1, :, at(h)] + half * (
                changes[1] - 2.0 * LOAD[h * rs : (h + 1) * rs, :]
            )

    def steel_stress():
        dr_x = rows_of(S, 0, steel_top, steel_bottom, lambda side: speed_rows.at[side, 0])
        dr_z = rows_of(S, 1, steel_top, steel_bottom, lambda side: speed_rows.at[side, 1])
        dc_x = columns(S, 0, rs, lambda side: speed_cols[side, 0])
        dc_z = columns(S, 1, rs, lambda side: speed_cols[side, 1])
        for h in range(nh):
            across, along = 0.5 * dr_x(h), 0.5 * dc_z(h)
            S[2, :, at(h)] = S[2, :, at(h)] + SC[1, :, at(h)] * across + SC[2, :, at(h)] * along
            S[3, :, at(h)] = S[3, :, at(h)] + SC[2, :, at(h)] * across + SC[3, :, at(h)] * along
            S[4, :, at(h)] = S[4, :, at(h)] + (0.5 * SC[4, :, at(h)]) * (dc_x(h) + dr_z(h))

    def water_part():
        dr_p = rows_of(W, 0, water_top, water_bottom)
        dc_p = columns(W, 0, rw)
        for h in range(nh):
            half = 0.5 * WC[0, :, at(h)]
            W[1, :, at(h)] = W[1, :, at(h)] - half * dr_p(h)
            W[2, :, at(h)] = W[2, :, at(h)] - half * dc_p(h)

    def water_rest(n):
        for side in (1, 0):
            near = p_rows_out[1 - side, n, 0]
            half = 0.5 * wcoef_rows_in[side, 0]
            vx_rows[side] = p_rows_in[side, n, 1] - half * (near if side else -near)
            half = 0.5 * wcoef_cols_in[side, 0]
            beside = forth(W[0, :, first]) if side else -back(W[0, :, last])
            vz_cols[side] = vz_cols_in[side, n, 0] - half * beside
        for h in range(nh):
            half = 0.5 * WC[0, :, at(h)]
            W[1, :, at(h)] = W[1, :, at(h)] - half * outside_rows(
                p_rows_in[1, n, 0, h : h + 1, :],
                p_rows_in[0, n, 0, h : h + 1, :],
                water_top,
                water_bottom,
            )
            if h in (0, nh - 1):
                W[2, :, at(h)] = W[2, :, at(h)] - half * outside_cols(
                    h, rw, p_cols_in[1, n, 0], p_cols_in[0, n, 0]
                )

    def water_pressure():
        dr_v = rows_of(W, 1, water_top, water_bottom, lambda side: vx_rows.at[side])
        dc_v = columns(W, 2, rw, lambda side: vz_cols[side])
        for h in range(nh):
            W[0, :, at(h)] = W[0, :, at(h)] - (0.5 * WC[1, :, at(h)]) * (dr_v(h) + dc_v(h))

    def water_feed(values):
        fed = scatter(values, RW, LW)
        for h in range(nh):
            W[0, :, at(h)] = W[0, :, at(h)] + fed[h * rw : (h + 1) * rw, :]

    def equal_cells(i, cells, start):
        for s0 in range(0, cap, LANES):
            block = cells[:, start + s0 : start + s0 + LANES]
            down = jnp.transpose(jnp.broadcast_to(block, (LANES, LANES)))
            for t0 in range(0, slots, LANES):
                same = down == cells[:, t0 : t0 + LANES]
                EQ[i, s0 : s0 + LANES, t0 : t0 + LANES] = jnp.where(same, 1.0, 0.0).astype(BF16)

    def fed_at_slots(i, values):
        high, low = split_two(values)
        upper = lax.broadcasted_iota(jnp.int32, (16, slots), 0) < 8
        both = jnp.where(upper, high.astype(F32), low.astype(F32)).astype(BF16)
        out = lax.dot_general(
            both, EQ[i], (((1,), (1,)), ((), ())), preferred_element_type=F32
        )
        return out[0:1] + out[8:9]

    loads[4].wait()
    sample = gather(W.at[0], rw, RW, LW) * FAC[...]
    known_out[0] = wcell.astype(F32)
    known_out[1] = FAC[...]
    loads[6].wait()
    loads[8].wait()
    put_stress(0)
    put_rows(lambda d: coef_rows_out.at[d], ((SC, 0),), rs)
    steel_part()
    put_part(0)
    loads[7].wait()
    put_p(0)
    put_rows(lambda d: wcoef_rows_out.at[d], ((WC, 0),), rw)
    water_part()
    put_vx(0)
    loads[5].wait()
    selectors(lane_row(steel_cell), rs, RS, LS)
    pl.semaphore_wait(barrier, sum(h.astype(jnp.int32) for h in has))
    send_lists("s0", 0, sample)
    for d in (0, 1):
        send("k", d, known_out, known_in.at[d])
    send_stress(0)
    send_part(0)
    all_rows("br", lambda d: coef_rows_out.at[d], lambda d: coef_rows_in.at[d])
    all_cols("bc", lambda e: SC.at[0:1, :, e], lambda d: coef_cols_in.at[d])
    send_p(0)
    all_rows("wr", lambda d: wcoef_rows_out.at[d], lambda d: wcoef_rows_in.at[d])
    all_cols("wc", lambda e: WC.at[0:1, :, e], lambda d: wcoef_cols_in.at[d])
    equal_cells(1, wcell.astype(F32), cap)
    wait_lists("s0", 0)
    loading = jnp.concatenate([lists_in[1, 0], sample[:, cap : 2 * cap], lists_in[0, 0]], axis=1)
    for d in (0, 1):
        arrived("k", d, known_in.at[d])
    equal_cells(0, known_in[1, 0], 2 * cap)
    equal_cells(2, known_in[0, 0], 0)
    for n in range(STEPS):
        LOAD[...] = scatter(loading, RS, LS)
        wait_steel(n)
        if n == 0:
            for d in (0, 1):
                arrived("br", d, coef_rows_in.at[d])
            for d in (2, 3):
                arrived("bc", d, coef_cols_in.at[d - 2])
        outer_speed(n)
        all_sent(f"uc{n}", (2, 3))
        steel_rest(n)
        all_sent(f"sc{n}", (2, 3))
        all_sent(f"sd{n}", range(4, 8))
        steel_stress()
        traction = gather(S.at[3], rs, RS, LS)
        send_tractions(n, traction)
        if n < STEPS - 1:
            put_stress(n + 1)
            send_stress(n + 1)
            steel_part()
            put_part(n + 1)
            send_part(n + 1)
        wait_water(n)
        if n == 0:
            for d in (0, 1):
                arrived("wr", d, wcoef_rows_in.at[d])
            for d in (2, 3):
                arrived("wc", d, wcoef_cols_in.at[d - 2])
        all_sent(f"vc{n}", (2, 3))
        water_rest(n)
        all_sent(f"pc{n}", (2, 3))
        water_pressure()
        if n < STEPS - 1:
            unfed = gather(W.at[0], rw, RW, LW)
            send_lists(f"q{n + 1}", n + 1, unfed)
        wait_tractions(n)
        own = FAC[...] * jnp.concatenate(
            [
                near_in[1, n][:, cap:],
                traction[:, cap : 2 * cap],
                near_in[0, n][:, :cap],
            ],
            axis=1,
        )
        water_feed(own)
        if n < STEPS - 1:
            put_p(n + 1)
            water_part()
            put_vx(n + 1)
            send_p(n + 1)
            before = known_in[1, 1] * jnp.concatenate(
                [far_in[1, n], near_in[1, n][:, :cap], traction[:, :cap]], axis=1
            )
            after = known_in[0, 1] * jnp.concatenate(
                [traction[:, 2 * cap :], near_in[0, n][:, cap:], far_in[0, n]], axis=1
            )
            fed = [fed_at_slots(i, v) for i, v in enumerate((before, own, after))]
            wait_lists(f"q{n + 1}", n + 1)
            loading = jnp.concatenate(
                [
                    known_in[1, 1][:, 2 * cap :] * (lists_in[1, n + 1] + fed[0]),
                    FAC[:, cap : 2 * cap] * (unfed[:, cap : 2 * cap] + fed[1]),
                    known_in[0, 1][:, :cap] * (lists_in[0, n + 1] + fed[2]),
                ],
                axis=1,
            )
    for name, d in list(pending):
        sent(name, d)


def store_kernel(water, steel, water_out, steel_out, sem):
    stores = [
        pltpu.make_async_copy(steel, steel_out, sem.at[0]),
        pltpu.make_async_copy(water, water_out, sem.at[1]),
    ]
    for store in stores:
        store.start()
    for store in stores:
        store.wait()


def on_device(
    tiles,
    subs,
    water_state,
    water_coef,
    steel_state,
    steel_coef,
    coupling,
    water_cell,
    stencil_code,
    link_count,
    steel_cell,
):
    rw, nz = water_state.shape[1:]
    rs = steel_state.shape[1]
    cap = water_cell.shape[1]
    slots = 3 * cap
    nh = nz // LANES
    vmem = pl.BlockSpec(memory_space=pltpu.VMEM)
    hbm = pl.BlockSpec(memory_space=pltpu.HBM)
    rows_of = lambda *lead: pltpu.VMEM((2, *lead, nh, LANES), F32)
    results = pl.pallas_call(
        functools.partial(kernel, (tiles, subs, rw, rs, nz, cap)),
        out_shape=(
            pltpu.VMEM(water_state.shape, F32),
            pltpu.VMEM(steel_state.shape, F32),
        ),
        in_specs=[hbm] * 9,
        out_specs=(vmem, vmem),
        scratch_shapes=[
            pltpu.SMEM(coupling.shape, F32),
            pltpu.SMEM((1, 3), jnp.int32),
            pltpu.VMEM(water_cell.shape, jnp.int32),
            pltpu.VMEM(water_cell.shape, jnp.int32),
            pltpu.VMEM(water_cell.shape, jnp.int32),
            pltpu.VMEM(water_coef.shape, F32),
            pltpu.VMEM(steel_coef.shape, F32),
            pltpu.VMEM((nh * rw, slots), BF16),
            pltpu.VMEM((nh * rs, slots), BF16),
            pltpu.VMEM((LANES, slots), F32),
            pltpu.VMEM((LANES, slots), F32),
            pltpu.VMEM((1, slots), F32),
            pltpu.VMEM((nh * rs, LANES), F32),
            pltpu.VMEM((3, cap, slots), BF16),
            pltpu.VMEM((2, STEPS, 1, cap), F32),
            pltpu.VMEM((2, STEPS, 1, cap), F32),
            pltpu.VMEM((2, STEPS, 1, 2 * cap), F32),
            pltpu.VMEM((2, STEPS, 1, 2 * cap), F32),
            pltpu.VMEM((2, STEPS, 1, cap), F32),
            pltpu.VMEM((2, STEPS, 1, cap), F32),
            pltpu.VMEM((2, 1, slots), F32),
            pltpu.VMEM((2, 2, 1, slots), F32),
            rows_of(STEPS, 2),
            rows_of(STEPS, 2),
            rows_of(STEPS, 2),
            rows_of(STEPS, 2),
            rows_of(1),
            rows_of(1),
            rows_of(2),
            rows_of(STEPS, 2),
            rows_of(STEPS, 2),
            rows_of(1),
            rows_of(1),
            rows_of(),
            pltpu.VMEM((2, STEPS, 2, rs, LANES), F32),
            pltpu.VMEM((2, STEPS, 2, rs, LANES), F32),
            pltpu.VMEM((2, 1, rs, LANES), F32),
            pltpu.VMEM((2, 2, rs, LANES), F32),
            pltpu.VMEM((2, STEPS, 1, rw, LANES), F32),
            pltpu.VMEM((2, STEPS, 1, rw, LANES), F32),
            pltpu.VMEM((2, 1, rw, LANES), F32),
            pltpu.VMEM((2, rw, LANES), F32),
            pltpu.VMEM((4, STEPS, 3, 8, LANES), F32),
            pltpu.SemaphoreType.DMA((9,)),
            pltpu.SemaphoreType.DMA((96,)),
            pltpu.SemaphoreType.DMA((96,)),
        ],
        compiler_params=pltpu.CompilerParams(
            collective_id=0, has_side_effects=True, vmem_limit_bytes=VMEM_BYTES - 4 * (water_state.size + steel_state.size)
        ),
    )(
        coupling,
        link_count.reshape(1, 3),
        water_cell,
        stencil_code,
        steel_cell,
        water_state,
        water_coef,
        steel_state,
        steel_coef,
    )
    return pl.pallas_call(
        store_kernel,
        out_shape=(
            jax.ShapeDtypeStruct(water_state.shape, F32),
            jax.ShapeDtypeStruct(steel_state.shape, F32),
        ),
        in_specs=[vmem, vmem],
        out_specs=(hbm, hbm),
        scratch_shapes=[pltpu.SemaphoreType.DMA((2,))],
        compiler_params=pltpu.CompilerParams(vmem_limit_bytes=1024 * 1024),
    )(*results)


def solution(mesh):
    in_specs = (
        P(None, "tile", "sub"),
        P(None, "tile", "sub"),
        P(None, "tile", "sub"),
        P(None, "tile", "sub"),
        P(),
        P("tile", "sub"),
        P("tile", "sub"),
        P("tile", "sub"),
        P("tile", "sub"),
    )
    out_specs = (P(None, "tile", "sub"), P(None, "tile", "sub"))
    return jax.shard_map(
        functools.partial(on_device, mesh.shape["tile"], mesh.shape["sub"]),
        mesh=mesh,
        in_specs=in_specs,
        out_specs=out_specs,
        check_vma=False,
    )
```
